256 devices in a mesh: sub: 32 (over x, z), crs: 8 (over y, core).
Axes of the slice: x: 4, y: 4, z: 8, core: 2. Of those that a mesh axis runs over, the one named last changes fastest.
Arguments:
- loads: float32 [128, 64, 1024], P('sub', None, 'crs'), may hold values from -6 to 6
- schur_blocks: float32 [128, 1024, 1024], P('sub', 'crs'), as said below
- coupling: float32 [128, 24, 1024], P('sub', None, 'crs'), may hold values from -0.3 to 0.3
- coarse_inverse: float32 [3072, 3072], P('crs'), as said below
- neighbours: int32 [128, 4], P('sub'), may hold values from 0 to 127, as said below
- face_len: int32 [128, 4], P('sub'), may hold values from 256 to 1024
- contact_pair: int32 [128], P('sub'), may hold values from 0 to 127, as said below
- stiffness: float32 [128], P('sub'), may hold values from 0.5 to 2
- scaling: float32 [128, 1024], P('sub', 'crs'), may hold values from 0.08 to 0.3
- corner_map: int32 [128, 24], P('sub'), may hold values from 0 to 3071
Outputs:
- solution: float32 [128, 64, 1024], P('sub', None, 'crs')
- residual: float32 [128, 64, 1024], P('sub', None, 'crs')
The draws below stay inside these ranges and needn't reach their ends.
Inputs may be any that keep to these rules, and one draw needn't show every extreme that they name: `neighbours`: for every slot the partner relation is an involution without fixed points and both partners have the same face_len; for slots 0 and 2 an even group of 4 consecutive subdomains pairs with the next group and an odd one with the previous group, for slots 1 and 3 the reverse, with wrap over the 128 subdomains. `contact_pair`: an involution; the partner lies in the group of 4 consecutive subdomains 128 // 2 subdomains away, with wrap. `schur_blocks`: each block is symmetric positive definite. `coarse_inverse`: symmetric positive definite.
All inputs are finite; a program needn't handle non-finite values.
Results may differ from the reference program's by a relative error of at most 0.0002.
Values sent between devices are 32-bit elements; how exact they have to be, the bound alone decides.
No kernel may reach another device: no remote copies, remote signals or barrier semaphores. Data moves between devices by JAX's collectives and lax.ppermute only.
A program may use at most 64 MiB of HBM per device.

```python
import math
import jax
import jax.numpy as jnp
from jax import lax

NI = 1024
NCO = 3072
NC = 24
FACES = 4
ITERS = 2
SUB_DEV = 4
NRHS = 64
SUBS = 128


def face_tables(key):
    group_count = SUBS // SUB_DEV
    groups = jnp.arange(group_count, dtype=jnp.int32)
    previous = (groups - 1) % group_count
    following = (groups + 1) % group_count
    partner_list = []
    length_list = []
    for face_slot in range(FACES):
        slot_key = jax.random.fold_in(key, 11 + face_slot)
        group_keys = jax.random.split(jax.random.fold_in(slot_key, 1), group_count)
        orders = jax.vmap(lambda one_key: jax.random.permutation(one_key, SUB_DEV))(group_keys).astype(jnp.int32)
        inverse = jnp.argsort(orders, axis=1).astype(jnp.int32)
        face_span = jax.random.randint(jax.random.fold_in(slot_key, 2), (group_count, SUB_DEV), NI // 4, NI + 1).astype(jnp.int32)
        if face_slot == 0:
            face_span = face_span.at[0, 0].set(NI)
        if face_slot == 1:
            face_span = face_span.at[1 % group_count, 0].set(NI // 4)
        leading = groups % 2 == face_slot % 2
        partner_lead = following[:, None] * SUB_DEV + orders
        partner_back = previous[:, None] * SUB_DEV + inverse[previous]
        partner = jnp.where(leading[:, None], partner_lead, partner_back)
        length_back = jnp.take_along_axis(face_span[previous], inverse[previous], axis=1)
        length = jnp.where(leading[:, None], face_span, length_back)
        partner_list.append(partner.reshape(SUBS))
        length_list.append(length.reshape(SUBS))
    return (jnp.stack(partner_list, axis=1).astype(jnp.int32), jnp.stack(length_list, axis=1).astype(jnp.int32))


def draw_neighbours(key, part):
    return face_tables(key)[0]


def draw_face_len(key, part):
    return face_tables(key)[1]


def draw_contact_pair(key, part):
    group_count = SUBS // SUB_DEV
    half_count = group_count // 2
    groups = jnp.arange(group_count, dtype=jnp.int32)
    group_keys = jax.random.split(jax.random.fold_in(key, 7), group_count)
    orders = jax.vmap(lambda one_key: jax.random.permutation(one_key, SUB_DEV))(group_keys).astype(jnp.int32)
    inverse = jnp.argsort(orders, axis=1).astype(jnp.int32)
    leading = groups < half_count
    opposite = (groups + half_count) % group_count
    partner = jnp.where(leading[:, None], opposite[:, None] * SUB_DEV + orders, opposite[:, None] * SUB_DEV + inverse[opposite])
    return partner.reshape(SUBS).astype(jnp.int32)


def draw_schur_blocks(key, part):
    noise = jnp.clip(jax.random.normal(jax.random.fold_in(key, 3), (SUBS, NI, NI), jnp.float32), -4.0, 4.0) * (0.7 / NI ** 0.5)
    return 4.0 * jnp.eye(NI, dtype=jnp.float32)[None, :, :] + noise + jnp.swapaxes(noise, 1, 2)


def draw_coarse_inverse(key, part):
    noise = jnp.clip(jax.random.normal(jax.random.fold_in(key, 5), (NCO, NCO), jnp.float32), -4.0, 4.0) * (0.6 / NCO ** 0.5)
    return 2.0 * jnp.eye(NCO, dtype=jnp.float32) + noise + noise.T


def place_ends(result, rng, low, top_value):
    index_at = [jax.random.randint(jax.random.fold_in(rng, axis), (), 0, length) for axis, length in enumerate(result.shape)]
    widest = result.shape.index(max(result.shape))
    next_to = index_at[:widest] + [(index_at[widest] + 1) % result.shape[widest]] + index_at[widest + 1:]
    return result.at[tuple(index_at)].set(low).at[tuple(next_to)].set(top_value)


def levels(key, extent, pieces, smallest, high):
    def one(dim, shards_of):
        heights = jax.random.uniform(jax.random.fold_in(jax.random.fold_in(key, 6), dim), (shards_of,), jnp.float32, smallest / len(pieces), high / len(pieces))
        return jnp.repeat(jnp.exp(heights), extent[dim] // shards_of).reshape((-1,) + (1,) * (len(extent) - dim - 1))

    level = one(*pieces[0])
    for cut in pieces[1:]:
        level = level * one(*cut)
    return level


def normal_values(own_key, shape, deviation, most, cuts=(), held_as=jnp.bfloat16):
    values = jax.random.normal(own_key, shape, jnp.float32) * deviation
    if len(cuts) > 0:
        values = levels(own_key, shape, cuts, -0.22, 0.18) * values
    return jnp.clip(values, min=-most, max=most).astype(held_as)


def setup_inputs(seed: int = 0) -> dict:
    keys = jax.random.split(jax.random.key(seed), 11)
    return {
        "loads": normal_values(keys[0], (SUBS, NRHS, NI), 1.0, 6.0, ((0, 32), (2, 8)), jnp.float32),
        "schur_blocks": draw_schur_blocks(jax.random.fold_in(keys[10], 71), 0),
        "coupling": normal_values(keys[2], (SUBS, NC, NI), 0.05, 0.3, ((0, 32), (2, 8)), jnp.float32),
        "coarse_inverse": draw_coarse_inverse(jax.random.fold_in(keys[10], 71), 0),
        "neighbours": draw_neighbours(jax.random.fold_in(keys[10], 71), 0),
        "face_len": draw_face_len(jax.random.fold_in(keys[10], 71), 0),
        "contact_pair": draw_contact_pair(jax.random.fold_in(keys[10], 71), 0),
        "stiffness": jnp.clip(jnp.exp(math.log(2.0) - 1.3862944 * jax.random.uniform(keys[7], (SUBS,), jnp.float32) ** levels(keys[7], (SUBS,), ((0, 32),), -0.2, 0.2)), 0.5, 2.0),
        "scaling": jnp.clip(jnp.exp(math.log(0.3) - 1.3217559 * jax.random.uniform(keys[8], (SUBS, NI), jnp.float32) ** levels(keys[8], (SUBS, NI), ((0, 32), (1, 8)), -0.2, 0.2)), 0.08, 0.3),
        "corner_map": place_ends(jax.random.randint(keys[9], (SUBS, NC), 0, NCO), jax.random.fold_in(keys[9], 1), 0, NCO - 1).astype(jnp.int32),
    }


HIGH = lax.Precision.HIGHEST


def schur_one(pair):
    return jnp.einsum('ik,rk->ri', pair[0], pair[1], precision=HIGH)


def apply_operator(field, schur_blocks, coupling, coarse_inverse, neighbours, face_len, contact_pair, stiffness, corner_map):
    schur_part = lax.map(schur_one, (schur_blocks, field))
    places = jnp.arange(NI, dtype=jnp.int32)
    jump_terms = jnp.zeros_like(field)
    for face_slot in range(FACES):
        live_mask = (places[None, :] < face_len[:, face_slot:face_slot + 1]).astype(jnp.float32)
        jump_terms = jump_terms + live_mask[:, None, :] * (field - field[neighbours[:, face_slot]])
    contact_weight = stiffness * stiffness[contact_pair]
    jump_terms = jump_terms + contact_weight[:, None, None] * (field - field[contact_pair])
    corner_part = jnp.einsum('snk,srk->rsn', coupling, field, precision=HIGH).reshape(NRHS, SUBS * NC)
    coarse_full = jnp.zeros((NRHS, NCO), jnp.float32).at[:, corner_map.reshape(-1)].add(corner_part)
    coarse_sol = jnp.dot(coarse_full, coarse_inverse.T, precision=HIGH)
    corner_vals = coarse_sol[:, corner_map]
    coarse_back = jnp.einsum('snk,rsn->srk', coupling, corner_vals, precision=HIGH)
    return schur_part + jump_terms + coarse_back


def reference(loads, schur_blocks, coupling, coarse_inverse, neighbours, face_len, contact_pair, stiffness, scaling, corner_map):
    solution = jnp.zeros_like(loads)
    residual = loads
    scaled = scaling[:, None, :] * residual
    direction = scaled
    norm_now = jnp.sum(residual * scaled, axis=(0, 2))
    for step_index in range(ITERS):
        image = apply_operator(direction, schur_blocks, coupling, coarse_inverse, neighbours, face_len, contact_pair, stiffness, corner_map)
        step_size = norm_now / jnp.sum(direction * image, axis=(0, 2))
        solution = solution + step_size[None, :, None] * direction
        residual = residual - step_size[None, :, None] * image
        if step_index + 1 < ITERS:
            scaled = scaling[:, None, :] * residual
            norm_next = jnp.sum(residual * scaled, axis=(0, 2))
            direction = scaled + (norm_next / norm_now)[None, :, None] * direction
            norm_now = norm_next
    return solution, residual
```

```python
import jax
import jax.numpy as jnp
from jax import lax
from jax.experimental import pallas as pl
from jax.experimental.pallas import tpu as pltpu
from jax.sharding import PartitionSpec as P

HIGH = lax.Precision.HIGH
HIGHEST = lax.Precision.HIGHEST
LANES = 128


def passed_along(value, axis, steps):
    count = lax.axis_size(axis)
    pairs = [(source, (source + steps) % count) for source in range(count)]
    return lax.ppermute(value, axis, pairs)


def to_everyone(value, axis):
    count = lax.axis_size(axis)
    copies = jnp.broadcast_to(value[None], (count, *value.shape))
    return lax.all_to_all(copies, axis, 0, 0, tiled=True)


def jump_kernel(is_next, row, length, weight, start, own, after, before, contact, out):
    subs, nrhs, columns = own.shape
    faces = length.shape[1]
    place = start[0] + lax.broadcasted_iota(jnp.int32, (nrhs, columns), 1)
    for s in range(subs):
        mine = own[s]
        total = weight[s] * (mine - contact[row[s, faces]])
        for f in range(faces):
            at = row[s, f]
            other = jnp.where(is_next[s, f] != 0, after[at], before[at])
            total = total + jnp.where(place < length[s, f], mine - other, 0.0)
        out[s] = total


def jump(tables, own, after, before, contact):
    smem = pl.BlockSpec(memory_space=pltpu.SMEM)
    vmem = pl.BlockSpec(memory_space=pltpu.VMEM)
    return pl.pallas_call(
        jump_kernel,
        out_shape=jax.ShapeDtypeStruct(own.shape, jnp.float32),
        in_specs=[smem] * 5 + [vmem] * 4,
        out_specs=vmem,
        name="jump",
    )(*tables, own, after, before, contact)


def local(
    loads,
    schur_blocks,
    coupling,
    coarse_inverse,
    neighbours,
    face_len,
    contact_pair,
    stiffness,
    scaling,
    corner_map,
):
    sub_dev, nrhs, columns = loads.shape
    corners = coupling.shape[1]
    listed = sub_dev * corners
    group_count = lax.axis_size("sub")
    parts = lax.axis_size("crs")
    my_group = lax.axis_index("sub")
    my_cols = lax.axis_index("crs")
    order = coarse_inverse.shape[1]
    share = nrhs // parts
    blocks = order // LANES

    own_map = jnp.pad(corner_map.reshape(-1), (0, LANES - listed), constant_values=-1)
    weights = scaling[:, None, :]
    first = weights * loads

    picker = (jnp.arange(order, dtype=jnp.int32)[:, None] == own_map[None, :]).astype(jnp.float32)
    inverse_part = jnp.dot(coarse_inverse, picker, precision=HIGHEST)
    inverse_cols = lax.all_gather(inverse_part, "crs", axis=0, tiled=True)

    partner_stiff = passed_along(stiffness, "sub", group_count // 2)
    partner_row = contact_pair % sub_dev
    partner_pick = (partner_row[:, None] == jnp.arange(sub_dev, dtype=jnp.int32)[None, :]).astype(
        jnp.float32
    )
    contact_weight = stiffness * jnp.sum(partner_pick * partner_stiff[None, :], axis=1)
    tables = (
        (neighbours // sub_dev == (my_group + 1) % group_count).astype(jnp.int32),
        jnp.concatenate([neighbours % sub_dev, partner_row[:, None]], axis=1),
        face_len,
        contact_weight,
        (my_cols * columns)[None],
    )

    def corner_sums(field, extras):
        part = jnp.einsum("snk,srk->rsn", coupling, field, precision=HIGHEST).reshape(nrhs, listed)
        cells = [part] + [extra[:, None] for extra in extras]
        wide = jnp.concatenate(cells, axis=1)
        wide = jnp.pad(wide, ((0, 0), (0, LANES - wide.shape[1])))
        sent = wide.reshape(parts, share, LANES)
        return jnp.sum(lax.all_to_all(sent, "crs", 0, 0, tiled=True), axis=0)

    def on_corners(gathered, all_map):
        high = all_map // LANES
        low = all_map % LANES
        rows = jnp.arange(blocks, dtype=jnp.int32)
        spread = jnp.where(
            high[None, None] == rows[None, :, None, None],
            gathered.transpose(1, 0, 2)[:, None],
            0.0,
        ).reshape(share * blocks, group_count * LANES)
        pick = (jnp.arange(LANES, dtype=jnp.int32)[:, None] == low.reshape(-1)[None, :]).astype(
            jnp.float32
        )
        full = lax.dot_general(spread, pick, (((1,), (1,)), ((), ())), precision=HIGHEST)
        return jnp.dot(full.reshape(share, order), inverse_cols, precision=HIGHEST)

    def back(rows):
        vals = rows[:, :listed].reshape(nrhs, sub_dev, corners)
        return jnp.einsum("snk,rsn->srk", coupling, vals, precision=HIGHEST)

    def near(field):
        whole = lax.all_gather(field, "crs", axis=2, tiled=True)
        after = passed_along(field, "sub", -1)
        before = passed_along(field, "sub", 1)
        contact = passed_along(field, "sub", group_count // 2)
        schur_part = jnp.einsum("sik,srk->sri", schur_blocks, whole, precision=HIGH)
        return schur_part + jump(tables, field, after, before, contact)

    norm_part = jnp.sum(loads * first, axis=(0, 2))
    first_sums = corner_sums(first, [norm_part])
    map_rows = jnp.broadcast_to(own_map.astype(jnp.float32)[None], (share, LANES))
    first_all = to_everyone(jnp.concatenate([first_sums, map_rows], axis=0), "sub")
    all_map = first_all[:, share].astype(jnp.int32)
    first_vals = on_corners(first_all[:, :share], all_map)
    near_first = near(first)
    first_rows = to_everyone(first_vals, "crs").reshape(nrhs, LANES)
    image = near_first + back(first_rows)

    second = weights * image
    curve_part = jnp.sum(first * image, axis=(0, 2))
    second_sums = corner_sums(second, [norm_part, curve_part])
    second_all = to_everyone(second_sums, "sub")
    second_vals = on_corners(second_all, all_map)
    dots = jnp.sum(second_all[:, :, listed : listed + 2], axis=0)
    second_vals = lax.dynamic_update_slice(second_vals, dots, (0, listed))
    near_second = near(second)
    second_rows = to_everyone(second_vals, "crs").reshape(nrhs, LANES)
    image_two = near_second + back(second_rows)

    norm = second_rows[:, listed]
    curve = second_rows[:, listed + 1]
    step = norm / curve
    wide_step = step[None, :, None]
    residual = loads - wide_step * image
    scaled = first - wide_step * second
    scaled_image = image - wide_step * image_two
    partial = jnp.stack(
        [
            jnp.sum(residual * scaled, axis=(0, 2)),
            jnp.sum(scaled * scaled_image, axis=(0, 2)),
            jnp.sum(scaled * image + first * scaled_image, axis=(0, 2)),
        ]
    )
    partial = jnp.pad(partial, ((0, 8 - partial.shape[0]), (0, LANES - nrhs)))
    partial = jnp.sum(to_everyone(partial, "crs"), axis=0)
    whole = jnp.sum(to_everyone(partial, "sub"), axis=0)[:, :nrhs]
    norm_next = whole[0]
    ratio = norm_next / norm
    curve_next = whole[1] + ratio * (whole[2] + ratio * curve)
    step_next = (norm_next / curve_next)[None, :, None]
    ratio = ratio[None, :, None]
    solution = wide_step * first + step_next * (scaled + ratio * first)
    residual = residual - step_next * (scaled_image + ratio * image)
    return (solution, residual)


def solution(mesh):
    return jax.shard_map(
        local,
        mesh=mesh,
        in_specs=(
            P("sub", None, "crs"),
            P("sub", "crs", None),
            P("sub", None, "crs"),
            P("crs", None),
            P("sub", None),
            P("sub", None),
            P("sub"),
            P("sub"),
            P("sub", "crs"),
            P("sub", None),
        ),
        out_specs=(P("sub", None, "crs"), P("sub", None, "crs")),
        check_vma=False,
    )
```

```python
import functools

import jax
import jax.numpy as jnp
from jax import lax
from jax.experimental import pallas as pl
from jax.experimental.pallas import tpu as pltpu
from jax.sharding import PartitionSpec as P

HIGH = lax.Precision.HIGH
HIGHEST = lax.Precision.HIGHEST
LANES = 128
CORES = 2
SMEM = pl.BlockSpec(memory_space=pltpu.SMEM)
VMEM = pl.BlockSpec(memory_space=pltpu.VMEM)
ROWS = (((1,), (1,)), ((), ()))


def along_sub(value, steps):
    count = lax.axis_size("sub")
    return lax.ppermute(value, "sub", [(s, (s + steps) % count) for s in range(count)])


def along_y(value, steps):
    count = lax.axis_size("crs")
    return lax.ppermute(value, "crs", [(s, (s + CORES * steps) % count) for s in range(count)])


def other_core(value):
    count = lax.axis_size("crs")
    return lax.ppermute(value, "crs", [(s, s ^ 1) for s in range(count)])


def exchange(value, axis):
    return lax.all_to_all(value, axis, 0, 0, tiled=True)


def to_everyone(value, axis):
    count = lax.axis_size(axis)
    return exchange(jnp.broadcast_to(value[None], (count, *value.shape)), axis)


def split(value):
    high = value.astype(jnp.bfloat16)
    low = (value - high.astype(jnp.float32)).astype(jnp.bfloat16)
    return high, low


def dot3(a, b, dims):
    a_high, a_low = split(a)
    b_high, b_low = split(b)

    def one(x, y):
        return lax.dot_general(x, y, dims, preferred_element_type=jnp.float32)

    return one(a_high, b_high) + (one(a_high, b_low) + one(a_low, b_high))


def coarse_kernel(listed, place, gathered, all_map, *refs):
    *columns, out, spread, pick = refs
    ys = len(columns)
    share = out.shape[0]
    groups = gathered.shape[0]
    blocks = columns[0].shape[0] // LANES
    half = ys * blocks * share
    sums = jnp.zeros((share, LANES), jnp.float32)
    for g in range(groups):
        lanes = slice(g * LANES, (g + 1) * LANES)
        corner = all_map[g : g + 1, :]
        high = lax.shift_right_arithmetic(corner, 7)
        low = lax.bitwise_and(corner, LANES - 1)
        mine = gathered[g, :share, :]
        sums = sums + mine
        upper = mine.astype(jnp.bfloat16).astype(jnp.float32)
        lower = mine - upper
        for d in range(ys):
            chunk = CORES * lax.rem(place[0] - d + ys, ys) + place[1]
            for j in range(blocks):
                row = (d * blocks + j) * share
                hit = high == blocks * chunk + j
                spread[row : row + share, lanes] = jnp.where(hit, upper, 0.0).astype(jnp.bfloat16)
                spread[half + row : half + row + share, lanes] = jnp.where(hit, lower, 0.0).astype(
                    jnp.bfloat16
                )
        at = lax.broadcasted_iota(jnp.int32, (LANES, LANES), 0) == low
        pick[:, lanes] = jnp.where(at, 1.0, 0.0).astype(jnp.bfloat16)
    full = lax.dot_general(spread[...], pick[...], ROWS, preferred_element_type=jnp.float32)
    full = full[:half] + full[half:]
    total = jnp.zeros((share, LANES), jnp.float32)
    for d in range(ys):
        for j in range(blocks):
            row = (d * blocks + j) * share
            total = total + dot3(
                full[row : row + share],
                columns[d][j * LANES : (j + 1) * LANES, :],
                (((1,), (0,)), ((), ())),
            )
    lane = lax.broadcasted_iota(jnp.int32, (share, LANES), 1)
    out[...] = jnp.where(lane < listed, total, sums / CORES)


def coarse_product(place, gathered, all_map, columns, share, listed):
    ys = len(columns)
    rows = 2 * ys * (columns[0].shape[0] // LANES) * share
    depth = gathered.shape[0] * LANES
    return pl.pallas_call(
        functools.partial(coarse_kernel, listed),
        out_shape=jax.ShapeDtypeStruct((share, LANES), jnp.float32),
        in_specs=[SMEM] + [VMEM] * (2 + ys),
        out_specs=VMEM,
        scratch_shapes=[
            pltpu.VMEM((rows, depth), jnp.bfloat16),
            pltpu.VMEM((LANES, depth), jnp.bfloat16),
        ],
        compiler_params=pltpu.CompilerParams(vmem_limit_bytes=32 << 20),
        name="coarse_product",
    )(place, gathered, all_map, *columns)


def near_kernel(
    place, is_next, row, length, weight, schur, same, cross, after, before, contact, scaling,
    coupling, out, corner,
):
    ys, subs, nrhs, columns = same.shape
    faces = length.shape[1]
    corners = coupling.shape[1]
    pos = (CORES * place[0] + place[1]) * columns + lax.broadcasted_iota(
        jnp.int32, (nrhs, columns), 1
    )
    lower_core = place[1] == 0
    dots = jnp.zeros((nrhs, 1), jnp.float32)
    sums = []
    for s in range(subs):
        mine = same[0, s]
        total = weight[s] * (mine - contact[row[s, faces]])
        for f in range(faces):
            at = row[s, f]
            other = jnp.where(is_next[s, f] != 0, after[at], before[at])
            total = total + jnp.where(pos < length[s, f], mine - other, 0.0)
        for d in range(ys):
            start = pl.multiple_of(lax.rem(place[0] - d + ys, ys) * (CORES * columns), LANES)
            a, b = same[d, s], cross[d, s]
            pair = jnp.concatenate(
                [jnp.where(lower_core, a, b), jnp.where(lower_core, b, a)], axis=1
            )
            total = total + dot3(pair, schur[s, :, pl.ds(start, CORES * columns)], ROWS)
        out[s] = total
        dots = dots + jnp.sum(mine * total, axis=1, keepdims=True)
        sums.append(dot3(scaling[s : s + 1, :] * total, coupling[s], ROWS))
    sums.append(dots)
    sums.append(jnp.zeros((nrhs, LANES - subs * corners - 1), jnp.float32))
    corner[...] = jnp.concatenate(sums, axis=1)


def near(place, tables, schur_blocks, field, scaling, coupling):
    ys = lax.axis_size("crs") // CORES
    same = jnp.stack([field] + [along_y(field, d) for d in range(1, ys)])
    cross = other_core(same)
    after = along_sub(field, -1)
    before = along_sub(field, 1)
    contact = along_sub(field, lax.axis_size("sub") // 2)
    return pl.pallas_call(
        near_kernel,
        out_shape=(
            jax.ShapeDtypeStruct(field.shape, jnp.float32),
            jax.ShapeDtypeStruct((field.shape[1], LANES), jnp.float32),
        ),
        in_specs=[SMEM] * 5 + [VMEM] * 8,
        out_specs=(VMEM, VMEM),
        compiler_params=pltpu.CompilerParams(vmem_limit_bytes=32 << 20),
        name="near",
    )(place, *tables, schur_blocks, same, cross, after, before, contact, scaling, coupling)


def local(
    loads,
    schur_blocks,
    coupling,
    coarse_inverse,
    neighbours,
    face_len,
    contact_pair,
    stiffness,
    scaling,
    corner_map,
):
    sub_dev, nrhs, columns = loads.shape
    corners = coupling.shape[1]
    listed = sub_dev * corners
    group_count = lax.axis_size("sub")
    parts = lax.axis_size("crs")
    ys = parts // CORES
    my_group = lax.axis_index("sub")
    my_cols = lax.axis_index("crs")
    order = coarse_inverse.shape[1]
    share = nrhs // ys
    place = jnp.stack([my_cols // CORES, my_cols % CORES]).astype(jnp.int32)

    own_map = jnp.pad(corner_map.reshape(-1), (0, LANES - listed), constant_values=-1)
    weights = scaling[:, None, :]
    first = weights * loads

    picker = (jnp.arange(order, dtype=jnp.int32)[:, None] == own_map[None, :]).astype(jnp.float32)
    inverse_part = jnp.dot(coarse_inverse, picker, precision=HIGH)
    inverse_cols = [inverse_part] + [along_y(inverse_part, d) for d in range(1, ys)]

    def by_load_case(wide):
        pieces = wide.reshape(ys, 1, share, LANES)
        return jnp.broadcast_to(pieces, (ys, CORES, share, LANES)).reshape(parts, share, LANES)

    norm_part = jnp.sum(loads * first, axis=(0, 2))
    part = jnp.einsum("snk,srk->rsn", coupling, first, precision=HIGH).reshape(nrhs, listed)
    wide = jnp.concatenate([part, norm_part[:, None]], axis=1)
    wide = jnp.pad(wide, ((0, 0), (0, LANES - listed - 1)))
    pairs = jnp.einsum("smk,snk->msn", coupling, coupling * weights, precision=HIGH)
    pairs = jnp.pad(pairs.reshape(corners, listed), ((0, 0), (0, LANES - listed)))
    sent = jnp.concatenate(
        [by_load_case(wide), jnp.broadcast_to(pairs[None], (parts, corners, LANES))], axis=1
    )
    got = jnp.sum(exchange(sent, "crs"), axis=0)
    first_sums = got[:share]
    pairs = got[share:, :listed].reshape(corners, sub_dev, corners)
    facts = jnp.stack(
        [own_map.astype(jnp.float32), jnp.pad(stiffness, (0, LANES - sub_dev))]
        + [jnp.zeros((LANES,), jnp.float32)] * 6
    )
    first_all = to_everyone(jnp.concatenate([first_sums, facts], axis=0), "sub")
    all_map = first_all[:, share].astype(jnp.int32)
    first_vals = coarse_product(place, first_all, all_map, inverse_cols, share, listed)

    partner_row = contact_pair % sub_dev
    partner_stiff = lax.dynamic_index_in_dim(
        first_all[:, share + 1, :sub_dev],
        (my_group + group_count // 2) % group_count,
        0,
        keepdims=False,
    )
    partner_pick = (partner_row[:, None] == jnp.arange(sub_dev, dtype=jnp.int32)[None, :]).astype(
        jnp.float32
    )
    contact_weight = stiffness * jnp.sum(partner_pick * partner_stiff[None, :], axis=1)
    tables = (
        (neighbours // sub_dev == (my_group + 1) % group_count).astype(jnp.int32),
        jnp.concatenate([neighbours % sub_dev, partner_row[:, None]], axis=1),
        face_len,
        contact_weight,
    )
    near_first, near_sums = near(place, tables, schur_blocks, first, scaling, coupling)

    sent = jnp.concatenate(
        [
            jnp.broadcast_to(first_vals[None], (parts, share, LANES)),
            by_load_case(near_sums),
        ],
        axis=1,
    )
    got = exchange(sent, "crs")

    def everyone(rows):
        return jnp.sum(rows.reshape(ys, CORES, share, LANES), axis=1).reshape(nrhs, LANES)

    def back(rows):
        vals = rows[:, :listed].reshape(nrhs, sub_dev, corners)
        return jnp.einsum("snk,rsn->srk", coupling, vals, precision=HIGH)

    first_rows = everyone(got[:, :share])
    mine = lax.dynamic_slice_in_dim(first_rows, place[0] * share, share, 0)[:, :listed]
    more = jnp.einsum(
        "msn,rsm->rsn", pairs, mine.reshape(share, sub_dev, corners), precision=HIGH
    ).reshape(share, listed)
    more_curve = jnp.sum(first_sums[:, :listed] * mine, axis=1, keepdims=True)
    more = jnp.concatenate([more, more_curve], axis=1)
    second_sums = jnp.sum(got[:, share:], axis=0) + jnp.pad(
        more, ((0, 0), (0, LANES - listed - 1))
    )
    second_all = to_everyone(second_sums, "sub")
    image = near_first + back(first_rows)
    second = weights * image
    second_vals = coarse_product(place, second_all, all_map, inverse_cols, share, listed)
    near_second, _ = near(place, tables, schur_blocks, second, scaling, coupling)
    second_rows = everyone(to_everyone(second_vals, "crs"))
    image_two = near_second + back(second_rows)

    norm = first_rows[:, listed]
    curve = second_rows[:, listed]
    step = norm / curve
    wide_step = step[None, :, None]
    residual = loads - wide_step * image
    scaled = first - wide_step * second
    scaled_image = image - wide_step * image_two
    partial = jnp.stack(
        [
            jnp.sum(residual * scaled, axis=(0, 2)),
            jnp.sum(scaled * scaled_image, axis=(0, 2)),
            jnp.sum(scaled * image + first * scaled_image, axis=(0, 2)),
        ]
    )
    partial = jnp.pad(partial, ((0, 8 - partial.shape[0]), (0, LANES - nrhs)))
    partial = jnp.sum(to_everyone(partial, "crs"), axis=0)
    whole = jnp.sum(to_everyone(partial, "sub"), axis=0)[:, :nrhs]
    norm_next = whole[0]
    ratio = norm_next / norm
    curve_next = whole[1] + ratio * (whole[2] + ratio * curve)
    step_next = (norm_next / curve_next)[None, :, None]
    ratio = ratio[None, :, None]
    solution = wide_step * first + step_next * (scaled + ratio * first)
    residual = residual - step_next * (scaled_image + ratio * image)
    return (solution, residual)


def solution(mesh):
    return jax.shard_map(
        local,
        mesh=mesh,
        in_specs=(
            P("sub", None, "crs"),
            P("sub", "crs", None),
            P("sub", None, "crs"),
            P("crs", None),
            P("sub", None),
            P("sub", None),
            P("sub"),
            P("sub"),
            P("sub", "crs"),
            P("sub", None),
        ),
        out_specs=(P("sub", None, "crs"), P("sub", None, "crs")),
        check_vma=False,
    )
```

```python
import functools

import jax
import jax.numpy as jnp
from jax import lax
from jax.experimental import pallas as pl
from jax.experimental.pallas import tpu as pltpu
from jax.sharding import PartitionSpec as P

HIGHEST = lax.Precision.HIGHEST
LANES = 128
SUBLANES = 8
CORES = 2
SMEM = pl.BlockSpec(memory_space=pltpu.SMEM)
VMEM = pl.BlockSpec(memory_space=pltpu.VMEM)
ROWS = (((1,), (1,)), ((), ()))
PLAIN = (((1,), (0,)), ((), ()))


def along_sub(value, steps):
    count = lax.axis_size("sub")
    return lax.ppermute(value, "sub", [(s, (s + steps) % count) for s in range(count)])


def along_y(value, steps):
    count = lax.axis_size("crs")
    return lax.ppermute(value, "crs", [(s, (s + CORES * steps) % count) for s in range(count)])


def other_core(value):
    count = lax.axis_size("crs")
    return lax.ppermute(value, "crs", [(s, s ^ 1) for s in range(count)])


def exchange(value, axis):
    return lax.all_to_all(value, axis, 0, 0, tiled=True)


def after_all(value, others):
    return lax.optimization_barrier((value, *others))[0]


def f32(*shape):
    return jax.ShapeDtypeStruct(shape, jnp.float32)


def call(kernel, name, out_shape, in_specs, operands, scratch=(), room=4):
    many = isinstance(out_shape, tuple)
    return pl.pallas_call(
        kernel,
        out_shape=out_shape,
        in_specs=in_specs,
        out_specs=(VMEM,) * len(out_shape) if many else VMEM,
        scratch_shapes=list(scratch),
        compiler_params=pltpu.CompilerParams(vmem_limit_bytes=room << 20),
        name=name,
    )(*operands)


def split(value):
    high = value.astype(jnp.bfloat16)
    low = (value - high.astype(jnp.float32)).astype(jnp.bfloat16)
    return high, low


def dot3(a, b, dims):
    rows = a.shape[0]
    a_high, a_low = split(a)
    b_high, b_low = split(b)
    both = jnp.concatenate([a_high, a_low], axis=0)
    by_high = lax.dot_general(both, b_high, dims, preferred_element_type=jnp.float32)
    by_low = lax.dot_general(a_high, b_low, dims, preferred_element_type=jnp.float32)
    return by_high[:rows] + (by_high[rows:] + by_low)


def lane_row(rows, lanes):
    return lax.broadcasted_iota(jnp.int32, (rows, lanes), 1)


def row_of(rows, lanes):
    return lax.broadcasted_iota(jnp.int32, (rows, lanes), 0)


def filled(pieces, rows):
    have = sum(piece.shape[1] for piece in pieces)
    return jnp.concatenate([*pieces, jnp.zeros((rows, LANES - have), jnp.float32)], axis=1)


def start_kernel(loads, scaling, coupling, first, sent):
    subs, nrhs, _ = loads.shape
    corners = coupling.shape[1]
    parts = sent.shape[0]
    share = nrhs * CORES // parts
    norm = jnp.zeros((nrhs, 1), jnp.float32)
    sums, pairs = [], []
    for s in range(subs):
        scale = scaling[s : s + 1, :]
        scaled = scale * loads[s]
        first[s] = scaled
        norm = norm + jnp.sum(loads[s] * scaled, axis=1, keepdims=True)
        sums.append(dot3(scaled, coupling[s], ROWS))
        pairs.append(dot3(coupling[s], scale * coupling[s], ROWS))
    wide = filled([*sums, norm], nrhs)
    pairs = filled(pairs, corners)
    for k in range(parts):
        y = k // CORES
        sent[k, :share, :] = wide[y * share : (y + 1) * share]
        sent[k, share:, :] = pairs


def choose_kernel(own_map, inverse, out):
    width = inverse.shape[1]
    base = pl.program_id(0) * width

    @pl.when(pl.program_id(0) == 0)
    def _():
        out[...] = jnp.zeros_like(out)

    hit = base + row_of(width, LANES) == own_map[...]
    pick = jnp.where(hit, 1.0, 0.0).astype(jnp.bfloat16)
    high, low = split(inverse[...])
    out[...] += lax.dot_general(high, pick, PLAIN, preferred_element_type=jnp.float32) + (
        lax.dot_general(low, pick, PLAIN, preferred_element_type=jnp.float32)
    )


def choose(own_map, inverse):
    rows, order = inverse.shape
    width = order // 4
    return pl.pallas_call(
        choose_kernel,
        out_shape=f32(rows, LANES),
        grid=(order // width,),
        in_specs=[
            pl.BlockSpec((1, LANES), lambda i: (0, 0)),
            pl.BlockSpec((rows, width), lambda i: (0, i)),
        ],
        out_specs=pl.BlockSpec((rows, LANES), lambda i: (0, 0)),
        compiler_params=pltpu.CompilerParams(vmem_limit_bytes=8 << 20),
        name="choose",
    )(own_map, inverse)


def first_message_kernel(got, own_map, out, kept):
    share = out.shape[1] - SUBLANES
    total = got[0]
    for k in range(1, got.shape[0]):
        total = total + got[k]
    kept[...] = total
    facts = jnp.broadcast_to(own_map[...].astype(jnp.float32), (SUBLANES, LANES))
    for g in range(out.shape[0]):
        out[g, :share, :] = total[:share]
        out[g, share:, :] = facts


def coarse_kernel(listed, share, place, gathered, first_all, *refs):
    *refs, out, spread, pick = refs
    ys = 4
    columns = refs[:ys]
    groups = gathered.shape[0]
    blocks = columns[0].shape[0] // LANES
    half = ys * blocks * share
    y, core = place[0], place[1]
    sums = jnp.zeros((share, LANES), jnp.float32)
    for g in range(groups):
        lanes = slice(g * LANES, (g + 1) * LANES)
        corner = first_all[g, share : share + 1, :].astype(jnp.int32)
        high = lax.shift_right_arithmetic(corner, 7)
        low = lax.bitwise_and(corner, LANES - 1)
        mine = gathered[g, :share, :]
        sums = sums + mine
        upper = mine.astype(jnp.bfloat16).astype(jnp.float32)
        lower = mine - upper
        for d in range(ys):
            chunk = CORES * lax.rem(y - d + ys, ys) + core
            for j in range(blocks):
                row = (d * blocks + j) * share
                hit = high == blocks * chunk + j
                spread[row : row + share, lanes] = jnp.where(hit, upper, 0.0).astype(jnp.bfloat16)
                spread[half + row : half + row + share, lanes] = jnp.where(hit, lower, 0.0).astype(
                    jnp.bfloat16
                )
        at = row_of(LANES, LANES) == low
        pick[:, lanes] = jnp.where(at, 1.0, 0.0).astype(jnp.bfloat16)
    full = lax.dot_general(spread[...], pick[...], ROWS, preferred_element_type=jnp.float32)
    full = full[:half] + full[half:]
    total = jnp.zeros((share, LANES), jnp.float32)
    for d in range(ys):
        row = d * blocks * share
        line = jnp.concatenate(
            [full[row + j * share : row + (j + 1) * share] for j in range(blocks)], axis=1
        )
        total = total + dot3(line, columns[d][...], PLAIN)
    total = jnp.where(lane_row(share, LANES) < listed, total, sums / CORES)
    for k in range(out.shape[0]):
        out[k, :share, :] = total
        if len(refs) > ys:
            at = k // CORES * share
            out[k, share:, :] = refs[ys][at : at + share, :]


def coarse_product(listed, share, place, gathered, first_all, columns, extra):
    rows = 2 * len(columns) * (columns[0].shape[0] // LANES) * share
    depth = gathered.shape[0] * LANES
    operands = [gathered, first_all, *columns, *extra]
    return call(
        functools.partial(coarse_kernel, listed, share),
        "coarse_product",
        f32(CORES * len(columns), share * (1 + len(extra)), LANES),
        [SMEM] + [VMEM] * len(operands),
        [place, *operands],
        [pltpu.VMEM((rows, depth), jnp.bfloat16), pltpu.VMEM((LANES, depth), jnp.bfloat16)],
        room=10,
    )


def near_kernel(
    faces, whole, factor, schur, same, cross, after, before, contact, *refs
):
    *refs, line = refs
    ys, subs, nrhs, columns = same.shape
    last = (2 * faces + 1) * subs
    y, core, group_after = whole[last], whole[last + 1], whole[last + 2]
    pos = (CORES * y + core) * columns + lane_row(nrhs, columns)
    lower_core = core == 0
    out = refs[2] if len(refs) > 1 else refs[0]
    dots = jnp.zeros((nrhs, 1), jnp.float32)
    sums = []
    for s in range(subs):
        for d in range(ys):
            start = pl.multiple_of(lax.rem(y - d + ys, ys) * (CORES * columns), LANES)
            a, b = same[d, s], cross[d, s]
            line[s, :, pl.ds(start, columns)] = jnp.where(lower_core, a, b)
            line[s, :, pl.ds(pl.multiple_of(start + columns, LANES), columns)] = jnp.where(
                lower_core, b, a
            )
    for s in range(subs):
        mine = same[0, s]
        at = lax.rem(whole[2 * faces * subs + s], subs)
        total = (factor[s] * factor[subs + at]) * (mine - contact[at])
        for f in range(faces):
            target = whole[s * faces + f]
            at = lax.rem(target, subs)
            is_after = lax.div(target, subs) == group_after
            other = jnp.where(is_after, after[at], before[at])
            live = pos < whole[(subs + s) * faces + f]
            total = total + jnp.where(live, mine - other, 0.0)
        total = total + dot3(line[s], schur[s], ROWS)
        out[s] = total
        if len(refs) > 1:
            scaling, coupling = refs[:2]
            dots = dots + jnp.sum(mine * total, axis=1, keepdims=True)
            sums.append(dot3(scaling[s : s + 1, :] * total, coupling[s], ROWS))
    if len(refs) > 1:
        refs[3][...] = filled([*sums, dots], nrhs)


def neighbourhood(field):
    ys = lax.axis_size("crs") // CORES
    same = jnp.stack([field] + [along_y(field, d) for d in range(1, ys)])
    return (
        same,
        other_core(same),
        along_sub(field, -1),
        along_sub(field, 1),
        along_sub(field, lax.axis_size("sub") // 2),
    )


def near_part(faces, tables, schur_blocks, around, extra):
    _, subs, nrhs, columns = around[0].shape
    field = f32(subs, nrhs, columns)
    return call(
        functools.partial(near_kernel, faces),
        "near",
        (field, f32(nrhs, LANES)) if extra else field,
        [SMEM] * len(tables) + [VMEM] * (1 + len(around) + len(extra)),
        [*tables, schur_blocks, *around, *extra],
        [pltpu.VMEM((subs, nrhs, schur_blocks.shape[2]), jnp.float32)],
        room=8,
    )


def second_message_kernel(listed, place, got, kept, out, rows):
    share = out.shape[1]
    parts = got.shape[0]
    corners = kept.shape[0] - share
    y = place[0]
    for k in range(parts // CORES):
        rows[k * share : (k + 1) * share, :] = (
            got[CORES * k, :share, :] + got[CORES * k + 1, :share, :]
        )
    mine = got[CORES * y, :share, :] + got[CORES * y + 1, :share, :]
    total = got[0, share:, :]
    for k in range(1, parts):
        total = total + got[k, share:, :]
    pairs = kept[share:, :]
    copies = jnp.concatenate([pairs] * (listed // corners), axis=0)
    whose = lax.div(row_of(listed, LANES), corners) == lax.div(lane_row(listed, LANES), corners)
    copies = jnp.where(whose, copies, 0.0)
    total = total + dot3(mine[:, :listed], copies, PLAIN)
    lane = lane_row(share, LANES)
    curve = jnp.where(lane < listed, kept[:share, :] * mine, 0.0)
    curve = jnp.sum(curve, axis=1, keepdims=True)
    total = total + jnp.where(lane == listed, curve, 0.0)
    for g in range(out.shape[0]):
        out[g] = total


def second_field_kernel(near_first, rows, coupling, scaling, image, second):
    subs = near_first.shape[0]
    corners = coupling.shape[1]
    for s in range(subs):
        vals = rows[:, s * corners : (s + 1) * corners]
        total = near_first[s] + dot3(vals, coupling[s], PLAIN)
        image[s] = total
        second[s] = scaling[s : s + 1, :] * total


def last_dots_kernel(
    got, rows, coupling, near_second, loads, first, image, second, sent, scaled_image, steps
):
    subs, nrhs, columns = loads.shape
    corners = coupling.shape[1]
    listed = subs * corners
    parts, share, _ = got.shape
    vals = jnp.concatenate(
        [got[CORES * k] + got[CORES * k + 1] for k in range(parts // CORES)], axis=0
    )
    norm = rows[:, listed : listed + 1]
    curve = vals[:, listed : listed + 1]
    step = norm / curve
    lane = lane_row(nrhs, LANES)
    steps[...] = jnp.where(lane == 0, norm, jnp.where(lane == 1, curve, step))
    products = [jnp.zeros((nrhs, columns), jnp.float32)] * 3
    for s in range(subs):
        image_two = near_second[s] + dot3(
            vals[:, s * corners : (s + 1) * corners], coupling[s], PLAIN
        )
        residual = loads[s] - step * image[s]
        scaled = first[s] - step * second[s]
        total = image[s] - step * image_two
        scaled_image[s] = total
        products = [
            products[0] + residual * scaled,
            products[1] + scaled * total,
            products[2] + (scaled * image[s] + first[s] * total),
        ]
    width = len(products) * columns
    chosen = lax.div(lane_row(SUBLANES, width), columns) == row_of(SUBLANES, width)
    sums = lax.dot_general(
        jnp.where(chosen, 1.0, 0.0),
        jnp.concatenate(products, axis=1),
        ROWS,
        precision=HIGHEST,
        preferred_element_type=jnp.float32,
    )
    sums = jnp.concatenate([sums, jnp.zeros((SUBLANES, LANES - nrhs), jnp.float32)], axis=1)
    for k in range(parts):
        sent[k] = sums


def last_message_kernel(got, out):
    total = got[0]
    for k in range(1, got.shape[0]):
        total = total + got[k]
    for g in range(out.shape[0]):
        out[g] = total


def last_kernel(
    got, steps, loads, first, image, second, scaled_image, solution_out, residual_out
):
    subs, nrhs, _ = loads.shape
    total = got[0]
    for g in range(1, got.shape[0]):
        total = total + got[g]
    same = jnp.where(row_of(nrhs, LANES) == lane_row(nrhs, LANES), 1.0, 0.0)
    sums = lax.dot_general(
        same, total, ROWS, precision=HIGHEST, preferred_element_type=jnp.float32
    )
    norm, curve, step = steps[:, 0:1], steps[:, 1:2], steps[:, 2:3]
    norm_next = sums[:, 0:1]
    ratio = norm_next / norm
    curve_next = sums[:, 1:2] + ratio * (sums[:, 2:3] + ratio * curve)
    step_next = norm_next / curve_next
    for s in range(subs):
        residual = loads[s] - step * image[s]
        scaled = first[s] - step * second[s]
        solution_out[s] = step * first[s] + step_next * (scaled + ratio * first[s])
        residual_out[s] = residual - step_next * (scaled_image[s] + ratio * image[s])


def local(
    loads,
    schur_blocks,
    coupling,
    coarse_inverse,
    neighbours,
    face_len,
    contact_pair,
    stiffness,
    scaling,
    corner_map,
):
    sub_dev, nrhs, columns = loads.shape
    corners = coupling.shape[1]
    listed = sub_dev * corners
    groups = lax.axis_size("sub")
    parts = lax.axis_size("crs")
    ys = parts // CORES
    share = nrhs // ys
    field = f32(sub_dev, nrhs, columns)

    my_cols = lax.axis_index("crs")
    group_after = (lax.axis_index("sub") + 1) % groups
    place = jnp.stack([my_cols // CORES, my_cols % CORES, group_after]).astype(jnp.int32)
    own_map = jnp.pad(corner_map.reshape(1, -1), ((0, 0), (0, LANES - listed)), constant_values=-1)
    tables = (
        jnp.concatenate([neighbours.reshape(-1), face_len.reshape(-1), contact_pair, place]),
        jnp.concatenate([stiffness, along_sub(stiffness, groups // 2)]),
    )
    near = functools.partial(near_part, neighbours.shape[1], tables, schur_blocks)

    first, sent = call(
        start_kernel,
        "start",
        (field, f32(parts, share + corners, LANES)),
        [VMEM] * 3,
        [loads, scaling, coupling],
    )
    around = neighbourhood(first)
    chosen = choose(after_all(own_map, [sent]), coarse_inverse)
    inverse_cols = [chosen] + [along_y(chosen, d) for d in range(1, ys)]
    got = exchange(sent, "crs")
    sent, kept = call(
        first_message_kernel,
        "first_message",
        (f32(groups, share + SUBLANES, LANES), f32(share + corners, LANES)),
        [VMEM] * 2,
        [got, own_map],
    )
    first_all = exchange(sent, "sub")
    around = lax.optimization_barrier((around, inverse_cols))[0]
    near_first, near_sums = near(around, (scaling, coupling))
    sent = coarse_product(listed, share, place, first_all, first_all, inverse_cols, (near_sums,))
    got = exchange(sent, "crs")
    sent, rows = call(
        functools.partial(second_message_kernel, listed),
        "second_message",
        (f32(groups, share, LANES), f32(nrhs, LANES)),
        [SMEM] + [VMEM] * 2,
        [place, got, kept],
    )
    second_all = exchange(sent, "sub")
    image, second = call(
        second_field_kernel,
        "second_field",
        (field, field),
        [VMEM] * 4,
        [near_first, rows, coupling, scaling],
    )
    around = neighbourhood(second)
    second_all = after_all(second_all, around[2:])
    sent = coarse_product(listed, share, place, second_all, first_all, inverse_cols, ())
    got = exchange(sent, "crs")
    near_second = near(around, ())
    sent, scaled_image, steps = call(
        last_dots_kernel,
        "last_dots",
        (f32(parts, SUBLANES, LANES), field, f32(nrhs, LANES)),
        [VMEM] * 8,
        [got, rows, coupling, near_second, loads, first, image, second],
    )
    got = exchange(sent, "crs")
    sent = call(last_message_kernel, "last_message", f32(groups, SUBLANES, LANES), [VMEM], [got])
    got = exchange(sent, "sub")
    return call(
        last_kernel,
        "last",
        (field, field),
        [VMEM] * 7,
        [got, steps, loads, first, image, second, scaled_image],
    )


def solution(mesh):
    return jax.shard_map(
        local,
        mesh=mesh,
        in_specs=(
            P("sub", None, "crs"),
            P("sub", "crs", None),
            P("sub", None, "crs"),
            P("crs", None),
            P("sub", None),
            P("sub", None),
            P("sub"),
            P("sub"),
            P("sub", "crs"),
            P("sub", None),
        ),
        out_specs=(P("sub", None, "crs"), P("sub", None, "crs")),
        check_vma=False,
    )
```

```python
import functools

import jax
import jax.numpy as jnp
from jax import lax
from jax.experimental import pallas as pl
from jax.experimental.pallas import tpu as pltpu
from jax.sharding import PartitionSpec as P

HIGHEST = lax.Precision.HIGHEST
LANES = 128
SUBLANES = 8
CORES = 2
SMEM = pl.BlockSpec(memory_space=pltpu.SMEM)
VMEM = pl.BlockSpec(memory_space=pltpu.VMEM)
ANY = pl.BlockSpec(memory_space=pl.ANY)
ROWS = (((1,), (1,)), ((), ()))
PLAIN = (((1,), (0,)), ((), ()))


def along_sub(value, steps):
    count = lax.axis_size("sub")
    return lax.ppermute(value, "sub", [(s, (s + steps) % count) for s in range(count)])


def along_y(value, steps):
    count = lax.axis_size("crs")
    return lax.ppermute(value, "crs", [(s, (s + CORES * steps) % count) for s in range(count)])


def other_core(value):
    count = lax.axis_size("crs")
    return lax.ppermute(value, "crs", [(s, s ^ 1) for s in range(count)])


def exchange(value, axis):
    return lax.all_to_all(value, axis, 0, 0, tiled=True)


def after_all(value, others):
    return lax.optimization_barrier((value, *others))[0]


def in_hbm(value):
    return pltpu.with_memory_space_constraint(value, pltpu.HBM)


def f32(*shape):
    return jax.ShapeDtypeStruct(shape, jnp.float32)


def call(kernel, name, out_shape, in_specs, operands, scratch=(), room=4):
    many = isinstance(out_shape, tuple)
    return pl.pallas_call(
        kernel,
        out_shape=out_shape,
        in_specs=in_specs,
        out_specs=(VMEM,) * len(out_shape) if many else VMEM,
        scratch_shapes=list(scratch),
        compiler_params=pltpu.CompilerParams(vmem_limit_bytes=room << 20),
        cost_estimate=pl.CostEstimate(flops=1 << 20, transcendentals=0, bytes_accessed=1 << 18),
        name=name,
    )(*operands)


def split(value):
    high = value.astype(jnp.bfloat16)
    low = (value - high.astype(jnp.float32)).astype(jnp.bfloat16)
    return high, low


def dot3(a, b, dims):
    rows = a.shape[0]
    a_high, a_low = split(a)
    b_high, b_low = split(b)
    both = jnp.concatenate([a_high, a_low], axis=0)
    by_high = lax.dot_general(both, b_high, dims, preferred_element_type=jnp.float32)
    by_low = lax.dot_general(a_high, b_low, dims, preferred_element_type=jnp.float32)
    return by_high[:rows] + (by_high[rows:] + by_low)


def lane_row(rows, lanes):
    return lax.broadcasted_iota(jnp.int32, (rows, lanes), 1)


def row_of(rows, lanes):
    return lax.broadcasted_iota(jnp.int32, (rows, lanes), 0)


def filled(pieces, rows):
    have = sum(piece.shape[1] for piece in pieces)
    return jnp.concatenate([*pieces, jnp.zeros((rows, LANES - have), jnp.float32)], axis=1)


def listed_row(corner_map):
    pieces = [corner_map[s : s + 1, :] for s in range(corner_map.shape[0])]
    have = sum(piece.shape[1] for piece in pieces)
    return jnp.concatenate([*pieces, jnp.full((1, LANES - have), -1, jnp.int32)], axis=1)


def start_kernel(
    loads_from, scaling_from, coupling_from, first, sent, stock, loads, scaling, coupling, arrived
):
    pairs = [(loads_from, loads), (scaling_from, scaling), (coupling_from, coupling)]
    copies = [pltpu.make_async_copy(*pair, arrived.at[i]) for i, pair in enumerate(pairs)]
    for copy in copies:
        copy.start()
    for copy in copies:
        copy.wait()
    subs, nrhs, _ = loads.shape
    corners = coupling.shape[1]
    parts = sent.shape[0]
    share = nrhs * CORES // parts
    norm = jnp.zeros((nrhs, 1), jnp.float32)
    sums, pairs = [], []
    for s in range(subs):
        scale = scaling[s : s + 1, :]
        scaled = scale * loads[s]
        first[s] = scaled
        stock[s, :nrhs, :] = loads[s]
        stock[s, nrhs : nrhs + corners, :] = coupling[s]
        stock[s, nrhs + corners :, :] = jnp.broadcast_to(scale, (SUBLANES, LANES))
        norm = norm + jnp.sum(loads[s] * scaled, axis=1, keepdims=True)
        sums.append(dot3(scaled, coupling[s], ROWS))
        pairs.append(dot3(coupling[s], scale * coupling[s], ROWS))
    wide = filled([*sums, norm], nrhs)
    pairs = filled(pairs, corners)
    for k in range(parts):
        y = k // CORES
        sent[k, :share, :] = wide[y * share : (y + 1) * share]
        sent[k, share:, :] = pairs


def choose_kernel(corner_map, inverse, out, pick):
    rows = inverse.shape[0]

    @pl.when(pl.program_id(0) == 0)
    def _():
        hit = row_of(*pick.shape) == listed_row(corner_map)
        pick[...] = jnp.where(hit, 1.0, 0.0).astype(jnp.bfloat16)

    both = jnp.concatenate(split(inverse[...]), axis=0)
    sums = lax.dot_general(both, pick[...], PLAIN, preferred_element_type=jnp.float32)
    out[...] = sums[:rows] + sums[rows:]


def choose(corner_map, inverse):
    rows, order = inverse.shape
    height = LANES
    return pl.pallas_call(
        choose_kernel,
        out_shape=f32(rows, LANES),
        grid=(rows // height,),
        in_specs=[
            pl.BlockSpec(corner_map.shape, lambda i: (0, 0)),
            pl.BlockSpec((height, order), lambda i: (i, 0)),
        ],
        out_specs=pl.BlockSpec((height, LANES), lambda i: (i, 0)),
        scratch_shapes=[pltpu.VMEM((order, LANES), jnp.bfloat16)],
        compiler_params=pltpu.CompilerParams(vmem_limit_bytes=12 << 20),
        name="choose",
    )(corner_map, in_hbm(inverse))


def first_message_kernel(place, stiffness, got, corner_map, out, kept):
    share = out.shape[1] - SUBLANES
    total = got[0]
    for k in range(1, got.shape[0]):
        total = total + got[k]
    kept[...] = total
    facts = [listed_row(corner_map).astype(jnp.float32)]
    for number in [place[i] for i in range(2)]:
        facts.append(jnp.full((1, LANES), number, jnp.int32).astype(jnp.float32))
    for s in range(stiffness.shape[0]):
        facts.append(jnp.full((1, LANES), stiffness[s], jnp.float32))
    facts.append(jnp.zeros((SUBLANES - len(facts), LANES), jnp.float32))
    facts = jnp.concatenate(facts, axis=0)
    for g in range(out.shape[0]):
        out[g, :share, :] = total[:share]
        out[g, share:, :] = facts


def coarse_kernel(listed, share, gathered, first_all, *refs):
    *refs, out, spread, pick, columns, arrived = refs
    ys = columns.shape[0]
    groups = gathered.shape[0]
    blocks = columns.shape[1] // LANES
    copies = [
        pltpu.make_async_copy(refs[d], columns.at[d], arrived.at[d]) for d in range(ys)
    ]
    for copy in copies:
        copy.start()
    half = ys * blocks * share
    y = first_all[0, share + 1 : share + 2, :].astype(jnp.int32)
    core = first_all[0, share + 2 : share + 3, :].astype(jnp.int32)
    sums = jnp.zeros((share, LANES), jnp.float32)
    targets = [
        blocks * (CORES * lax.bitwise_and(y - d + ys, ys - 1) + core) + j
        for d in range(ys)
        for j in range(blocks)
    ]
    for g in range(groups):
        lanes = slice(g * LANES, (g + 1) * LANES)
        corner = first_all[g, share : share + 1, :].astype(jnp.int32)
        high = lax.shift_right_arithmetic(corner, 7)
        low = lax.bitwise_and(corner, LANES - 1)
        mine = gathered[g, :share, :]
        sums = sums + mine
        upper = mine.astype(jnp.bfloat16).astype(jnp.float32)
        lower = mine - upper
        for block, target in enumerate(targets):
            row = block * share
            hit = high == target
            spread[row : row + share, lanes] = jnp.where(hit, upper, 0.0).astype(jnp.bfloat16)
            spread[half + row : half + row + share, lanes] = jnp.where(hit, lower, 0.0).astype(
                jnp.bfloat16
            )
        at = row_of(LANES, LANES) == low
        pick[:, lanes] = jnp.where(at, 1.0, 0.0).astype(jnp.bfloat16)
    full = lax.dot_general(spread[...], pick[...], ROWS, preferred_element_type=jnp.float32)
    full = full[:half] + full[half:]
    total = jnp.zeros((share, LANES), jnp.float32)
    for copy in copies:
        copy.wait()
    for d in range(ys):
        row = d * blocks * share
        line = jnp.concatenate(
            [full[row + j * share : row + (j + 1) * share] for j in range(blocks)], axis=1
        )
        total = total + dot3(line, columns[d][...], PLAIN)
    total = jnp.where(lane_row(share, LANES) < listed, total, sums / CORES)
    for k in range(out.shape[0]):
        out[k, :share, :] = total
        if len(refs) > ys:
            at = k // CORES * share
            out[k, share:, :] = refs[ys][refs[ys].shape[0] - 2, at : at + share, :]


def coarse_product(listed, share, gathered, first_all, columns, extra):
    rows = 2 * len(columns) * (columns[0].shape[0] // LANES) * share
    depth = gathered.shape[0] * LANES
    operands = [gathered, first_all, *[in_hbm(part) for part in columns], *extra]
    return call(
        functools.partial(coarse_kernel, listed, share),
        "coarse_product",
        f32(CORES * len(columns), share * (1 + len(extra)), LANES),
        [VMEM] * 2 + [ANY] * len(columns) + [VMEM] * len(extra),
        operands,
        [
            pltpu.VMEM((rows, depth), jnp.bfloat16),
            pltpu.VMEM((LANES, depth), jnp.bfloat16),
            pltpu.VMEM((len(columns), *columns[0].shape), jnp.float32),
            pltpu.SemaphoreType.DMA((len(columns),)),
        ],
        room=10,
    )


def near_kernel(faces, share, with_sums, whole, schur, first_all, stock, *refs):
    *blocks, after_from, before_from, contact_from, out, line, after, before, contact, arrived = refs
    subs, nrhs, columns = after.shape
    ys = len(blocks) // CORES
    corners = stock.shape[1] - nrhs - SUBLANES
    last = (2 * faces + 1) * subs
    y, core, group_after = whole[last], whole[last + 1], whole[last + 2]
    mine_at, partner_at = whole[last + 3], whole[last + 4]
    own = CORES * y + core
    pos = own * columns + lane_row(nrhs, columns)
    count = len(blocks)
    near_by = [(after_from, after), (before_from, before), (contact_from, contact)]
    near_by = [
        pltpu.make_async_copy(*pair, arrived.at[count + i]) for i, pair in enumerate(near_by)
    ]
    copies = []
    for i, block in enumerate(blocks):
        d, other = i % ys, i // ys
        chunk = CORES * lax.rem(y - d + ys, ys) + (1 - core if other else core)
        lanes = pl.ds(pl.multiple_of(chunk * columns, LANES), columns)
        copies.append(pltpu.make_async_copy(block, line.at[:, :, lanes], arrived.at[i]))
    for copy in [copies[0], *near_by, *copies[1:]]:
        copy.start()
    for copy in [copies[0], *near_by]:
        copy.wait()
    dots = jnp.zeros((nrhs, 1), jnp.float32)
    sums = []
    for s in range(subs):
        mine = line[s, :, pl.ds(pl.multiple_of(own * columns, LANES), columns)]
        at = lax.rem(whole[2 * faces * subs + s], subs)
        ours = first_all[mine_at, pl.ds(share + 3 + s, 1), :]
        theirs = first_all[partner_at, pl.ds(share + 3 + at, 1), :]
        total = (ours * theirs) * (mine - contact[at])
        for f in range(faces):
            target = whole[s * faces + f]
            at = lax.rem(target, subs)
            is_after = lax.div(target, subs) == group_after
            other = jnp.where(is_after, after[at], before[at])
            live = pos < whole[(subs + s) * faces + f]
            total = total + jnp.where(live, mine - other, 0.0)
        out[s] = total
    for copy in copies[1:]:
        copy.wait()
    for s in range(subs):
        mine = line[s, :, pl.ds(pl.multiple_of(own * columns, LANES), columns)]
        total = out[s] + dot3(line[s], schur[s], ROWS)
        out[s] = total
        if with_sums:
            dots = dots + jnp.sum(mine * total, axis=1, keepdims=True)
            scale = stock[s, nrhs + corners : nrhs + corners + 1, :]
            sums.append(dot3(scale * total, stock[s, nrhs : nrhs + corners, :], ROWS))
    if with_sums:
        out[subs] = filled([*sums, dots], nrhs)
        out[subs + 1] = jnp.zeros((nrhs, LANES), jnp.float32)


def neighbourhood(field):
    ys = lax.axis_size("crs") // CORES
    same = [field] + [along_y(field, d) for d in range(1, ys)]
    cross = [other_core(part) for part in same]
    return (
        *same,
        *cross,
        along_sub(field, -1),
        along_sub(field, 1),
        along_sub(field, lax.axis_size("sub") // 2),
    )


def near_part(faces, share, whole, schur_blocks, first_all, stock, around, with_sums):
    subs, nrhs, columns = around[0].shape
    piece = pltpu.VMEM((subs, nrhs, columns), jnp.float32)
    return call(
        functools.partial(near_kernel, faces, share, with_sums),
        "near",
        f32(subs + 2 * with_sums, nrhs, columns),
        [SMEM] + [VMEM] * 3 + [ANY] * len(around),
        [whole, schur_blocks, first_all, stock, *[in_hbm(part) for part in around]],
        [
            pltpu.VMEM((subs, nrhs, schur_blocks.shape[2]), jnp.float32),
            piece,
            piece,
            piece,
            pltpu.SemaphoreType.DMA((len(around),)),
        ],
        room=8,
    )


def second_message_kernel(
    listed, got, kept, first_all, near_first, first, stock, out, second, fields, rows
):
    share = out.shape[1]
    parts = got.shape[0]
    subs, nrhs, _ = first.shape
    corners = kept.shape[0] - share
    y = first_all[0, share + 1 : share + 2, :].astype(jnp.int32)
    mine = jnp.zeros((share, LANES), jnp.float32)
    for k in range(parts // CORES):
        vals = got[CORES * k, :share, :] + got[CORES * k + 1, :share, :]
        rows[k * share : (k + 1) * share, :] = vals
        mine = jnp.where(y == k, vals, mine)
    total = got[0, share:, :]
    for k in range(1, parts):
        total = total + got[k, share:, :]
    pairs = kept[share:, :]
    copies = jnp.concatenate([pairs] * (listed // corners), axis=0)
    whose = lax.div(row_of(listed, LANES), corners) == lax.div(lane_row(listed, LANES), corners)
    copies = jnp.where(whose, copies, 0.0)
    total = total + dot3(mine[:, :listed], copies, PLAIN)
    lane = lane_row(share, LANES)
    curve = jnp.where(lane < listed, kept[:share, :] * mine, 0.0)
    curve = jnp.sum(curve, axis=1, keepdims=True)
    total = total + jnp.where(lane == listed, curve, 0.0)
    for g in range(out.shape[0]):
        out[g] = total
    for s in range(subs):
        vals = rows[:, s * corners : (s + 1) * corners]
        image = near_first[s] + dot3(vals, stock[s, nrhs : nrhs + corners, :], PLAIN)
        scaled = stock[s, nrhs + corners : nrhs + corners + 1, :] * image
        second[s] = scaled
        fields[s] = first[s]
        fields[subs + s] = image
        fields[2 * subs + s] = scaled


def last_dots_kernel(
    got, rows, near_second, stock, fields, sent, scaled_image, steps
):
    subs, nrhs, columns = near_second.shape
    corners = stock.shape[1] - nrhs - SUBLANES
    listed = subs * corners
    parts, share, _ = got.shape
    vals = jnp.concatenate(
        [got[CORES * k] + got[CORES * k + 1] for k in range(parts // CORES)], axis=0
    )
    norm = rows[:, listed : listed + 1]
    curve = vals[:, listed : listed + 1]
    step = norm / curve
    lane = lane_row(nrhs, LANES)
    steps[...] = jnp.where(lane == 0, norm, jnp.where(lane == 1, curve, step))
    products = [jnp.zeros((nrhs, columns), jnp.float32)] * 3
    for s in range(subs):
        image_two = near_second[s] + dot3(
            vals[:, s * corners : (s + 1) * corners], stock[s, nrhs : nrhs + corners, :], PLAIN
        )
        first, image = fields[s], fields[subs + s]
        residual = stock[s, :nrhs, :] - step * image
        scaled = first - step * fields[2 * subs + s]
        total = image - step * image_two
        scaled_image[s] = total
        products = [
            products[0] + residual * scaled,
            products[1] + scaled * total,
            products[2] + (scaled * image + first * total),
        ]
    width = len(products) * columns
    chosen = lax.div(lane_row(SUBLANES, width), columns) == row_of(SUBLANES, width)
    sums = lax.dot_general(
        jnp.where(chosen, 1.0, 0.0),
        jnp.concatenate(products, axis=1),
        ROWS,
        precision=HIGHEST,
        preferred_element_type=jnp.float32,
    )
    sums = jnp.concatenate([sums, jnp.zeros((SUBLANES, LANES - nrhs), jnp.float32)], axis=1)
    for k in range(parts):
        sent[k] = sums


def last_message_kernel(got, out):
    total = got[0]
    for k in range(1, got.shape[0]):
        total = total + got[k]
    for g in range(out.shape[0]):
        out[g] = total


def last_kernel(got, steps, stock, fields, scaled_image, solution_out, residual_out):
    subs, nrhs, _ = scaled_image.shape
    total = got[0]
    for g in range(1, got.shape[0]):
        total = total + got[g]
    same = jnp.where(row_of(nrhs, LANES) == lane_row(nrhs, LANES), 1.0, 0.0)
    sums = lax.dot_general(
        same, total, ROWS, precision=HIGHEST, preferred_element_type=jnp.float32
    )
    norm, curve, step = steps[:, 0:1], steps[:, 1:2], steps[:, 2:3]
    norm_next = sums[:, 0:1]
    ratio = norm_next / norm
    curve_next = sums[:, 1:2] + ratio * (sums[:, 2:3] + ratio * curve)
    step_next = norm_next / curve_next
    for s in range(subs):
        first, image = fields[s], fields[subs + s]
        residual = stock[s, :nrhs, :] - step * image
        scaled = first - step * fields[2 * subs + s]
        solution_out[s] = step * first + step_next * (scaled + ratio * first)
        residual_out[s] = residual - step_next * (scaled_image[s] + ratio * image)


def local(
    loads,
    schur_blocks,
    coupling,
    coarse_inverse,
    neighbours,
    face_len,
    contact_pair,
    stiffness,
    scaling,
    corner_map,
):
    sub_dev, nrhs, columns = loads.shape
    corners = coupling.shape[1]
    listed = sub_dev * corners
    groups = lax.axis_size("sub")
    parts = lax.axis_size("crs")
    ys = parts // CORES
    share = nrhs // ys
    field = f32(sub_dev, nrhs, columns)

    my_cols = lax.axis_index("crs")
    my_group = lax.axis_index("sub")
    place = jnp.stack(
        [
            my_cols // CORES,
            my_cols % CORES,
            (my_group + 1) % groups,
            my_group,
            (my_group + groups // 2) % groups,
        ]
    ).astype(jnp.int32)
    whole = jnp.concatenate([neighbours.reshape(-1), face_len.reshape(-1), contact_pair, place])

    first, sent, stock = call(
        start_kernel,
        "start",
        (
            field,
            f32(parts, share + corners, LANES),
            f32(sub_dev, nrhs + corners + SUBLANES, columns),
        ),
        [ANY] * 3,
        [in_hbm(loads), in_hbm(scaling), in_hbm(coupling)],
        [pltpu.VMEM(part.shape, jnp.float32) for part in (loads, scaling, coupling)]
        + [pltpu.SemaphoreType.DMA((3,))],
    )
    chosen = choose(after_all(corner_map, [sent]), coarse_inverse)
    got = after_all(exchange(sent, "crs"), [chosen])
    sent, kept = call(
        first_message_kernel,
        "first_message",
        (f32(groups, share + SUBLANES, LANES), f32(share + corners, LANES)),
        [SMEM] * 2 + [VMEM] * 2,
        [place, stiffness, got, corner_map],
    )
    chosen = after_all(chosen, [kept])
    inverse_cols = [chosen] + [along_y(chosen, d) for d in range(1, ys)]
    around = neighbourhood(after_all(first, [kept]))
    first_all = exchange(sent, "sub")
    near = functools.partial(
        near_part, neighbours.shape[1], share, whole, schur_blocks, first_all, stock
    )
    near_first = near(around, True)
    sent = coarse_product(listed, share, first_all, first_all, inverse_cols, (near_first,))
    got = exchange(sent, "crs")
    sent, second, fields, rows = call(
        functools.partial(second_message_kernel, listed),
        "second_message",
        (f32(groups, share, LANES), field, f32(3 * sub_dev, nrhs, columns), f32(nrhs, LANES)),
        [VMEM] * 6,
        [got, kept, first_all, near_first, first, stock],
    )
    second_all = exchange(sent, "sub")
    around = neighbourhood(second)
    second_all = after_all(second_all, around[-3:])
    sent = coarse_product(listed, share, second_all, first_all, inverse_cols, ())
    got = exchange(sent, "crs")
    near_second = near(around, False)
    sent, scaled_image, steps = call(
        last_dots_kernel,
        "last_dots",
        (f32(parts, SUBLANES, LANES), field, f32(nrhs, LANES)),
        [VMEM] * 5,
        [got, rows, near_second, stock, fields],
    )
    got = exchange(sent, "crs")
    sent = call(last_message_kernel, "last_message", f32(groups, SUBLANES, LANES), [VMEM], [got])
    got = exchange(sent, "sub")
    return call(
        last_kernel,
        "last",
        (field, field),
        [VMEM] * 5,
        [got, steps, stock, fields, scaled_image],
    )


def solution(mesh):
    return jax.shard_map(
        local,
        mesh=mesh,
        in_specs=(
            P("sub", None, "crs"),
            P("sub", "crs", None),
            P("sub", None, "crs"),
            P("crs", None),
            P("sub", None),
            P("sub", None),
            P("sub"),
            P("sub"),
            P("sub", "crs"),
            P("sub", None),
        ),
        out_specs=(P("sub", None, "crs"), P("sub", None, "crs")),
        check_vma=False,
    )
```

```python
import functools

import jax
import jax.numpy as jnp
from jax import lax
from jax.experimental import pallas as pl
from jax.experimental.pallas import tpu as pltpu
from jax.sharding import PartitionSpec as P

HIGHEST = lax.Precision.HIGHEST
LANES = 128
SUBLANES = 8
CORES = 2
SMEM = pl.BlockSpec(memory_space=pltpu.SMEM)
VMEM = pl.BlockSpec(memory_space=pltpu.VMEM)
ANY = pl.BlockSpec(memory_space=pl.ANY)
ROWS = (((1,), (1,)), ((), ()))
PLAIN = (((1,), (0,)), ((), ()))


def along_sub(value, steps):
    count = lax.axis_size("sub")
    return lax.ppermute(value, "sub", [(s, (s + steps) % count) for s in range(count)])


def along_y(value, steps):
    count = lax.axis_size("crs")
    return lax.ppermute(value, "crs", [(s, (s + CORES * steps) % count) for s in range(count)])


def other_core(value):
    count = lax.axis_size("crs")
    return lax.ppermute(value, "crs", [(s, s ^ 1) for s in range(count)])


def exchange(value, axis):
    return lax.all_to_all(value, axis, 0, 0, tiled=True)


def after_all(value, others):
    return lax.optimization_barrier((value, *others))[0]


def in_hbm(value):
    return pltpu.with_memory_space_constraint(value, pltpu.HBM)


def f32(*shape):
    return jax.ShapeDtypeStruct(shape, jnp.float32)


def call(kernel, name, out_shape, in_specs, operands, scratch=(), room=4):
    many = isinstance(out_shape, tuple)
    return pl.pallas_call(
        kernel,
        out_shape=out_shape,
        in_specs=in_specs,
        out_specs=(VMEM,) * len(out_shape) if many else VMEM,
        scratch_shapes=list(scratch),
        compiler_params=pltpu.CompilerParams(vmem_limit_bytes=room << 20),
        cost_estimate=pl.CostEstimate(flops=1 << 20, transcendentals=0, bytes_accessed=1 << 18),
        name=name,
    )(*operands)


def split(value):
    high = value.astype(jnp.bfloat16)
    low = (value - high.astype(jnp.float32)).astype(jnp.bfloat16)
    return high, low


def dot3(a, b, dims):
    rows = a.shape[0]
    a_high, a_low = split(a)
    b_high, b_low = split(b)
    both = jnp.concatenate([a_high, a_low], axis=0)
    by_high = lax.dot_general(both, b_high, dims, preferred_element_type=jnp.float32)
    by_low = lax.dot_general(a_high, b_low, dims, preferred_element_type=jnp.float32)
    return by_high[:rows] + (by_high[rows:] + by_low)


def two_sum(a, b):
    total = a + b
    part = total - a
    return total, (a - (total - part)) + (b - part)


def two_product(a, b):
    def halves(x):
        big = x * 4097.0
        high = big - (big - x)
        return high, x - high

    product = a * b
    a_high, a_low = halves(a)
    b_high, b_low = halves(b)
    error = ((a_high * b_high - product) + a_high * b_low + a_low * b_high) + a_low * b_low
    return product, error


def pair_sum(a, b):
    total, error = two_sum(a[0], b[0])
    return two_sum(total, error + (a[1] + b[1]))


def pair_product(a, b):
    product, error = two_product(a[0], b[0])
    return two_sum(product, error + (a[0] * b[1] + a[1] * b[0]))


def scaled_pair(a, factor):
    return a[0] * factor, a[1] * factor


def lane_row(rows, lanes):
    return lax.broadcasted_iota(jnp.int32, (rows, lanes), 1)


def row_of(rows, lanes):
    return lax.broadcasted_iota(jnp.int32, (rows, lanes), 0)


def filled(pieces, rows):
    have = sum(piece.shape[1] for piece in pieces)
    return jnp.concatenate([*pieces, jnp.zeros((rows, LANES - have), jnp.float32)], axis=1)


def listed_row(corner_map):
    pieces = [corner_map[s : s + 1, :] for s in range(corner_map.shape[0])]
    have = sum(piece.shape[1] for piece in pieces)
    return jnp.concatenate([*pieces, jnp.full((1, LANES - have), -1, jnp.int32)], axis=1)


def start_kernel(
    loads_from, scaling_from, coupling_from, first, sent, stock, loads, scaling, coupling, arrived
):
    pairs = [(loads_from, loads), (scaling_from, scaling), (coupling_from, coupling)]
    copies = [pltpu.make_async_copy(*pair, arrived.at[i]) for i, pair in enumerate(pairs)]
    for copy in copies:
        copy.start()
    for copy in copies:
        copy.wait()
    subs, nrhs, _ = loads.shape
    corners = coupling.shape[1]
    parts = sent.shape[0]
    share = nrhs * CORES // parts
    norm = jnp.zeros((nrhs, 1), jnp.float32)
    sums, pairs = [], []
    for s in range(subs):
        scale = scaling[s : s + 1, :]
        scaled = scale * loads[s]
        first[s] = scaled
        stock[s, :nrhs, :] = loads[s]
        stock[s, nrhs : nrhs + corners, :] = coupling[s]
        stock[s, nrhs + corners :, :] = jnp.broadcast_to(scale, (SUBLANES, LANES))
        norm = norm + jnp.sum(loads[s] * scaled, axis=1, keepdims=True)
        sums.append(dot3(scaled, coupling[s], ROWS))
        pairs.append(dot3(coupling[s], scale * coupling[s], ROWS))
    wide = filled([*sums, norm], nrhs)
    pairs = filled(pairs, corners)
    for k in range(parts):
        y = k // CORES
        sent[k, :share, :] = wide[y * share : (y + 1) * share]
        sent[k, share:, :] = pairs


def choose_kernel(corner_map, inverse, out, pick):
    rows = inverse.shape[0]

    @pl.when(pl.program_id(0) == 0)
    def _():
        hit = row_of(*pick.shape) == listed_row(corner_map)
        pick[...] = jnp.where(hit, 1.0, 0.0).astype(jnp.bfloat16)

    both = jnp.concatenate(split(inverse[...]), axis=0)
    sums = lax.dot_general(both, pick[...], PLAIN, preferred_element_type=jnp.float32)
    out[...] = sums[:rows] + sums[rows:]


def choose(corner_map, inverse):
    rows, order = inverse.shape
    height = LANES
    return pl.pallas_call(
        choose_kernel,
        out_shape=f32(rows, LANES),
        grid=(rows // height,),
        in_specs=[
            pl.BlockSpec(corner_map.shape, lambda i: (0, 0)),
            pl.BlockSpec((height, order), lambda i: (i, 0)),
        ],
        out_specs=pl.BlockSpec((height, LANES), lambda i: (i, 0)),
        scratch_shapes=[pltpu.VMEM((order, LANES), jnp.bfloat16)],
        compiler_params=pltpu.CompilerParams(vmem_limit_bytes=12 << 20),
        name="choose",
    )(corner_map, in_hbm(inverse))


def first_message_kernel(place, stiffness, got, corner_map, out, kept):
    share = out.shape[1] - SUBLANES
    total = got[0]
    for k in range(1, got.shape[0]):
        total = total + got[k]
    kept[...] = total
    facts = [listed_row(corner_map).astype(jnp.float32)]
    for number in [place[i] for i in range(2)]:
        facts.append(jnp.full((1, LANES), number, jnp.int32).astype(jnp.float32))
    for s in range(stiffness.shape[0]):
        facts.append(jnp.full((1, LANES), stiffness[s], jnp.float32))
    facts.append(jnp.zeros((SUBLANES - len(facts), LANES), jnp.float32))
    facts = jnp.concatenate(facts, axis=0)
    for g in range(out.shape[0]):
        out[g, :share, :] = total[:share]
        out[g, share:, :] = facts


def coarse_kernel(listed, share, gathered, first_all, *refs):
    *refs, out, spread, pick, columns, arrived = refs
    ys = columns.shape[0]
    groups = gathered.shape[0]
    blocks = columns.shape[1] // LANES
    copies = [
        pltpu.make_async_copy(refs[d], columns.at[d], arrived.at[d]) for d in range(ys)
    ]
    for copy in copies:
        copy.start()
    half = ys * blocks * share
    y = first_all[0, share + 1 : share + 2, :].astype(jnp.int32)
    core = first_all[0, share + 2 : share + 3, :].astype(jnp.int32)
    sums = (jnp.zeros((share, LANES), jnp.float32),) * 2
    targets = [
        blocks * (CORES * lax.bitwise_and(y - d + ys, ys - 1) + core) + j
        for d in range(ys)
        for j in range(blocks)
    ]
    for g in range(groups):
        lanes = slice(g * LANES, (g + 1) * LANES)
        corner = first_all[g, share : share + 1, :].astype(jnp.int32)
        high = lax.shift_right_arithmetic(corner, 7)
        low = lax.bitwise_and(corner, LANES - 1)
        mine = gathered[g, :share, :]
        most, rest = two_sum(sums[0], mine)
        sums = most, sums[1] + rest
        upper = mine.astype(jnp.bfloat16).astype(jnp.float32)
        lower = mine - upper
        for block, target in enumerate(targets):
            row = block * share
            hit = high == target
            spread[row : row + share, lanes] = jnp.where(hit, upper, 0.0).astype(jnp.bfloat16)
            spread[half + row : half + row + share, lanes] = jnp.where(hit, lower, 0.0).astype(
                jnp.bfloat16
            )
        at = row_of(LANES, LANES) == low
        pick[:, lanes] = jnp.where(at, 1.0, 0.0).astype(jnp.bfloat16)
    full = lax.dot_general(spread[...], pick[...], ROWS, preferred_element_type=jnp.float32)
    full = full[:half] + full[half:]
    total = jnp.zeros((share, LANES), jnp.float32)
    for copy in copies:
        copy.wait()
    for d in range(ys):
        row = d * blocks * share
        line = jnp.concatenate(
            [full[row + j * share : row + (j + 1) * share] for j in range(blocks)], axis=1
        )
        total = total + dot3(line, columns[d][...], PLAIN)
    lane = lane_row(share, LANES)
    most, rest = (jnp.sum(jnp.where(lane == listed, x, 0.0), axis=1, keepdims=True) for x in sums)
    answer = jnp.where(lane < listed, total, 0.0)
    total = answer + jnp.where(lane == listed, most / CORES, 0.0)
    total = total + jnp.where(lane == listed + 1, rest / CORES, 0.0)
    for k in range(out.shape[0]):
        out[k, :share, :] = total
    if len(refs) == ys:
        out[0, share:, :] = jnp.zeros((out.shape[1] - share, LANES), jnp.float32)
    else:
        near_part = refs[ys]
        for k in range(out.shape[0]):
            at = k // CORES * share
            out[k, share:, :] = near_part[near_part.shape[0] - 2, at : at + share, :]


def coarse_product(listed, share, gathered, first_all, columns, extra):
    rows = 2 * len(columns) * (columns[0].shape[0] // LANES) * share
    depth = gathered.shape[0] * LANES
    operands = [gathered, first_all, *[in_hbm(part) for part in columns], *extra]
    return call(
        functools.partial(coarse_kernel, listed, share),
        "coarse_product",
        f32(CORES * len(columns) if extra else 1, 2 * share, LANES),
        [VMEM] * 2 + [ANY] * len(columns) + [VMEM] * len(extra),
        operands,
        [
            pltpu.VMEM((rows, depth), jnp.bfloat16),
            pltpu.VMEM((LANES, depth), jnp.bfloat16),
            pltpu.VMEM((len(columns), *columns[0].shape), jnp.float32),
            pltpu.SemaphoreType.DMA((len(columns),)),
        ],
        room=10,
    )


def row_sums(products):
    nrhs, columns = products[0].shape
    width = len(products) * columns
    chosen = lax.div(lane_row(SUBLANES, width), columns) == row_of(SUBLANES, width)
    sums = lax.dot_general(
        jnp.where(chosen, 1.0, 0.0),
        jnp.concatenate(products, axis=1),
        ROWS,
        precision=HIGHEST,
        preferred_element_type=jnp.float32,
    )
    return jnp.concatenate([sums, jnp.zeros((SUBLANES, LANES - nrhs), jnp.float32)], axis=1)


def near_kernel(faces, share, with_sums, whole, schur, first_all, stock, *refs):
    if with_sums:
        *refs, out, line, after, before, contact, arrived = refs
    else:
        answer, rows, fields, *refs, out, sent, line, after, before, contact, arrived = refs
    *blocks, after_from, before_from, contact_from = refs
    subs, nrhs, columns = after.shape
    ys = len(blocks) // CORES
    corners = stock.shape[1] - nrhs - SUBLANES
    last = (2 * faces + 1) * subs
    y, core, group_after = whole[last], whole[last + 1], whole[last + 2]
    mine_at, partner_at = whole[last + 3], whole[last + 4]
    own = CORES * y + core
    pos = own * columns + lane_row(nrhs, columns)
    count = len(blocks)
    near_by = [(after_from, after), (before_from, before), (contact_from, contact)]
    near_by = [
        pltpu.make_async_copy(*pair, arrived.at[count + i]) for i, pair in enumerate(near_by)
    ]
    copies = []
    for i, block in enumerate(blocks):
        d, other = i % ys, i // ys
        chunk = CORES * lax.rem(y - d + ys, ys) + (1 - core if other else core)
        lanes = pl.ds(pl.multiple_of(chunk * columns, LANES), columns)
        copies.append(pltpu.make_async_copy(block, line.at[:, :, lanes], arrived.at[i]))
    for copy in [copies[0], *near_by, *copies[1:]]:
        copy.start()
    for copy in [copies[0], *near_by]:
        copy.wait()
    dots = jnp.zeros((nrhs, 1), jnp.float32)
    sums = []
    products = [jnp.zeros((nrhs, columns), jnp.float32)] * 2
    for s in range(subs):
        mine = line[s, :, pl.ds(pl.multiple_of(own * columns, LANES), columns)]
        at = lax.rem(whole[2 * faces * subs + s], subs)
        ours = first_all[mine_at, pl.ds(share + 3 + s, 1), :]
        theirs = first_all[partner_at, pl.ds(share + 3 + at, 1), :]
        total = (ours * theirs) * (mine - contact[at])
        for f in range(faces):
            target = whole[s * faces + f]
            at = lax.rem(target, subs)
            is_after = lax.div(target, subs) == group_after
            other = jnp.where(is_after, after[at], before[at])
            live = pos < whole[(subs + s) * faces + f]
            total = total + jnp.where(live, mine - other, 0.0)
        out[s] = total
    for copy in copies[1:]:
        copy.wait()
    for s in range(subs):
        mine = line[s, :, pl.ds(pl.multiple_of(own * columns, LANES), columns)]
        total = out[s] + dot3(line[s], schur[s], ROWS)
        out[s] = total
        if with_sums:
            dots = dots + jnp.sum(mine * total, axis=1, keepdims=True)
            scale = stock[s, nrhs + corners : nrhs + corners + 1, :]
            sums.append(dot3(scale * total, stock[s, nrhs : nrhs + corners, :], ROWS))
        else:
            products = [products[0] + mine * fields[subs + s], products[1] + mine * total]
    if with_sums:
        out[subs] = filled([*sums, dots], nrhs)
        out[subs + 1] = jnp.zeros((nrhs, LANES), jnp.float32)
    else:
        answer = answer[0, :share, :]
        ours = jnp.where(lane_row(share, LANES) < subs * corners, answer, 0.0)
        ones = jnp.ones((SUBLANES, LANES), jnp.float32)
        dots = lax.dot_general(
            ones,
            rows[nrhs:, :] * ours,
            ROWS,
            precision=HIGHEST,
            preferred_element_type=jnp.float32,
        )
        dots = jnp.concatenate([dots] * (LANES // share), axis=1)
        dots = jnp.where(lax.div(lane_row(SUBLANES, LANES), share) == y, dots, 0.0)
        dots = jnp.where(row_of(SUBLANES, LANES) == 1, dots, 0.0)
        dots = row_sums(products) + dots
        for k in range(sent.shape[0]):
            sent[k, :share, :] = answer
            sent[k, share:, :] = dots


def neighbourhood(field):
    ys = lax.axis_size("crs") // CORES
    same = [field] + [along_y(field, d) for d in range(1, ys)]
    cross = [other_core(part) for part in same]
    return (
        *same,
        *cross,
        along_sub(field, -1),
        along_sub(field, 1),
        along_sub(field, lax.axis_size("sub") // 2),
    )


def near_part(faces, share, whole, schur_blocks, first_all, stock, around, with_sums, *extra):
    subs, nrhs, columns = around[0].shape
    piece = pltpu.VMEM((subs, nrhs, columns), jnp.float32)
    return call(
        functools.partial(near_kernel, faces, share, with_sums),
        "near",
        f32(subs + 2, nrhs, columns)
        if with_sums
        else (
            f32(subs, nrhs, columns),
            f32(schur_blocks.shape[2] // columns, share + SUBLANES, LANES),
        ),
        [SMEM] + [VMEM] * (3 + len(extra)) + [ANY] * len(around),
        [whole, schur_blocks, first_all, stock, *extra, *[in_hbm(part) for part in around]],
        [
            pltpu.VMEM((subs, nrhs, schur_blocks.shape[2]), jnp.float32),
            piece,
            piece,
            piece,
            pltpu.SemaphoreType.DMA((len(around),)),
        ],
        room=8,
    )


def second_message_kernel(
    listed, got, kept, first_all, near_from, first, stock, out, second, fields, rows, near_first,
    arrived,
):
    subs = first.shape[0]
    copy = pltpu.make_async_copy(near_from.at[pl.ds(0, subs)], near_first, arrived.at[0])
    copy.start()
    share = out.shape[1]
    parts = got.shape[0]
    subs, nrhs, _ = first.shape
    corners = kept.shape[0] - share
    y = first_all[0, share + 1 : share + 2, :].astype(jnp.int32)
    mine = jnp.zeros((share, LANES), jnp.float32)
    for k in range(parts // CORES):
        vals = got[CORES * k, :share, :] + got[CORES * k + 1, :share, :]
        rows[k * share : (k + 1) * share, :] = vals
        mine = jnp.where(y == k, vals, mine)
    total = got[0, share:, :]
    for k in range(1, parts):
        total = total + got[k, share:, :]
    pairs = kept[share:, :]
    copies = jnp.concatenate([pairs] * (listed // corners), axis=0)
    whose = lax.div(row_of(listed, LANES), corners) == lax.div(lane_row(listed, LANES), corners)
    copies = jnp.where(whose, copies, 0.0)
    total = total + dot3(mine[:, :listed], copies, PLAIN)
    lane = lane_row(share, LANES)
    curve = jnp.where(lane < listed, kept[:share, :] * mine, 0.0)
    curve = jnp.sum(curve, axis=1, keepdims=True)
    total = total + jnp.where(lane == listed, curve, 0.0)
    for g in range(out.shape[0]):
        out[g] = total
    rows[nrhs:, :] = total
    copy.wait()
    for s in range(subs):
        vals = rows[:nrhs, s * corners : (s + 1) * corners]
        image = near_first[s] + dot3(vals, stock[s, nrhs : nrhs + corners, :], PLAIN)
        scaled = stock[s, nrhs + corners : nrhs + corners + 1, :] * image
        second[s] = scaled
        fields[s] = first[s]
        fields[subs + s] = image
        fields[2 * subs + s] = scaled


def last_message_kernel(got, out, vals):
    parts = got.shape[0]
    share = vals.shape[0] * CORES // parts
    total = got[0, share:, :]
    for k in range(1, parts):
        total = total + got[k, share:, :]
    for g in range(out.shape[0]):
        out[g] = total
    for k in range(parts // CORES):
        vals[k * share : (k + 1) * share, :] = (
            got[CORES * k, :share, :] + got[CORES * k + 1, :share, :]
        )


def last_field_kernel(vals, near_second, stock, out):
    nrhs = vals.shape[0]
    corners = stock.shape[1] - nrhs - SUBLANES
    for s in range(stock.shape[0]):
        out[s] = near_second[s] + dot3(
            vals[:, s * corners : (s + 1) * corners], stock[s, nrhs : nrhs + corners, :], PLAIN
        )


def last_kernel(listed, got, rows, vals, stock, fields, image_two, solution_out, residual_out):
    subs, nrhs, _ = image_two.shape
    total = got[0], jnp.zeros_like(got[0])
    for g in range(1, got.shape[0]):
        most, rest = two_sum(total[0], got[g])
        total = most, total[1] + rest
    same = jnp.where(row_of(nrhs, LANES) == lane_row(nrhs, LANES), 1.0, 0.0)
    columns = lax.dot_general(
        same,
        jnp.concatenate(total, axis=0),
        ROWS,
        precision=HIGHEST,
        preferred_element_type=jnp.float32,
    )
    at = listed
    norm = two_sum(rows[:nrhs, at : at + 1], rows[:nrhs, at + 1 : at + 2])
    curve = two_sum(vals[:, at : at + 1], vals[:, at + 1 : at + 2])
    cross = two_sum(columns[:, 0:1], columns[:, SUBLANES : SUBLANES + 1])
    last = two_sum(columns[:, 1:2], columns[:, SUBLANES + 1 : SUBLANES + 2])
    zero = jnp.zeros_like(norm[0])
    step = norm[0] / curve[0]
    wide = step, zero
    moved = pair_product(wide, cross)
    norm_next = pair_sum(
        norm, pair_product(wide, pair_sum(moved, scaled_pair(curve, -2.0)))
    )
    ratio = norm_next[0] / norm[0]
    more = two_sum(jnp.ones_like(ratio), ratio)
    curve_next = pair_product(more, pair_sum(pair_product(more, curve), scaled_pair(moved, -2.0)))
    curve_next = pair_sum(curve_next, pair_product(wide, pair_product(wide, last)))
    step_next = norm_next[0] / curve_next[0]
    for s in range(subs):
        first, image = fields[s], fields[subs + s]
        residual = stock[s, :nrhs, :] - step * image
        scaled = first - step * fields[2 * subs + s]
        scaled_image = image - step * image_two[s]
        solution_out[s] = step * first + step_next * (scaled + ratio * first)
        residual_out[s] = residual - step_next * (scaled_image + ratio * image)


def local(
    loads,
    schur_blocks,
    coupling,
    coarse_inverse,
    neighbours,
    face_len,
    contact_pair,
    stiffness,
    scaling,
    corner_map,
):
    sub_dev, nrhs, columns = loads.shape
    corners = coupling.shape[1]
    listed = sub_dev * corners
    groups = lax.axis_size("sub")
    parts = lax.axis_size("crs")
    ys = parts // CORES
    share = nrhs // ys
    field = f32(sub_dev, nrhs, columns)

    my_cols = lax.axis_index("crs")
    my_group = lax.axis_index("sub")
    place = jnp.stack(
        [
            my_cols // CORES,
            my_cols % CORES,
            (my_group + 1) % groups,
            my_group,
            (my_group + groups // 2) % groups,
        ]
    ).astype(jnp.int32)
    whole = jnp.concatenate([neighbours.reshape(-1), face_len.reshape(-1), contact_pair, place])

    first, sent, stock = call(
        start_kernel,
        "start",
        (
            field,
            f32(parts, share + corners, LANES),
            f32(sub_dev, nrhs + corners + SUBLANES, columns),
        ),
        [ANY] * 3,
        [in_hbm(loads), in_hbm(scaling), in_hbm(coupling)],
        [pltpu.VMEM(part.shape, jnp.float32) for part in (loads, scaling, coupling)]
        + [pltpu.SemaphoreType.DMA((3,))],
    )
    chosen = choose(after_all(corner_map, [sent]), coarse_inverse)
    got = after_all(exchange(sent, "crs"), [chosen])
    sent, kept = call(
        first_message_kernel,
        "first_message",
        (f32(groups, share + SUBLANES, LANES), f32(share + corners, LANES)),
        [SMEM] * 2 + [VMEM] * 2,
        [place, stiffness, got, corner_map],
    )
    chosen = after_all(chosen, [kept])
    inverse_cols = [chosen] + [along_y(chosen, d) for d in range(1, ys)]
    around = neighbourhood(after_all(first, [kept]))
    first_all = exchange(sent, "sub")
    near = functools.partial(
        near_part, neighbours.shape[1], share, whole, schur_blocks, first_all, stock
    )
    near_first = near(around, True)
    sent = coarse_product(listed, share, first_all, first_all, inverse_cols, (near_first,))
    got = exchange(sent, "crs")
    sent, second, fields, rows = call(
        functools.partial(second_message_kernel, listed),
        "second_message",
        (
            f32(groups, share, LANES),
            field,
            f32(3 * sub_dev, nrhs, columns),
            f32(nrhs + share, LANES),
        ),
        [VMEM] * 3 + [ANY] + [VMEM] * 2,
        [got, kept, first_all, in_hbm(near_first), first, stock],
        [pltpu.VMEM((sub_dev, nrhs, columns), jnp.float32), pltpu.SemaphoreType.DMA((1,))],
    )
    second_all = exchange(sent, "sub")
    around = neighbourhood(second)
    answer = coarse_product(listed, share, second_all, first_all, inverse_cols, ())
    near_second, sent = near(around, False, answer, rows, fields)
    got = exchange(sent, "crs")
    sent, vals = call(
        last_message_kernel,
        "last_message",
        (f32(groups, SUBLANES, LANES), f32(nrhs, LANES)),
        [VMEM],
        [got],
    )
    got = exchange(sent, "sub")
    image_two = call(last_field_kernel, "last_field", field, [VMEM] * 3, [vals, near_second, stock])
    return call(
        functools.partial(last_kernel, listed),
        "last",
        (field, field),
        [VMEM] * 6,
        [got, rows, vals, stock, fields, image_two],
    )


def solution(mesh):
    return jax.shard_map(
        local,
        mesh=mesh,
        in_specs=(
            P("sub", None, "crs"),
            P("sub", "crs", None),
            P("sub", None, "crs"),
            P("crs", None),
            P("sub", None),
            P("sub", None),
            P("sub"),
            P("sub"),
            P("sub", "crs"),
            P("sub", None),
        ),
        out_specs=(P("sub", None, "crs"), P("sub", None, "crs")),
        check_vma=False,
    )
```

```python
import functools

import jax
import jax.numpy as jnp
from jax import lax
from jax.experimental import pallas as pl
from jax.experimental.pallas import tpu as pltpu
from jax.sharding import PartitionSpec as P

HIGHEST = lax.Precision.HIGHEST
LANES = 128
SUBLANES = 8
CORES = 2
SMEM = pl.BlockSpec(memory_space=pltpu.SMEM)
VMEM = pl.BlockSpec(memory_space=pltpu.VMEM)
ANY = pl.BlockSpec(memory_space=pl.ANY)
ROWS = (((1,), (1,)), ((), ()))
PLAIN = (((1,), (0,)), ((), ()))


def along_sub(value, steps):
    count = lax.axis_size("sub")
    return lax.ppermute(value, "sub", [(s, (s + steps) % count) for s in range(count)])


def along_y(value, steps):
    count = lax.axis_size("crs")
    return lax.ppermute(value, "crs", [(s, (s + CORES * steps) % count) for s in range(count)])


def other_core(value):
    count = lax.axis_size("crs")
    return lax.ppermute(value, "crs", [(s, s ^ 1) for s in range(count)])


def exchange(value, axis):
    return lax.all_to_all(value, axis, 0, 0, tiled=True)


def after_all(value, others):
    return lax.optimization_barrier((value, *others))[0]


def in_hbm(value):
    return pltpu.with_memory_space_constraint(value, pltpu.HBM)


def f32(*shape):
    return jax.ShapeDtypeStruct(shape, jnp.float32)


def call(kernel, name, out_shape, in_specs, operands, scratch=(), room=4, out_specs=None):
    many = isinstance(out_shape, tuple)
    return pl.pallas_call(
        kernel,
        out_shape=out_shape,
        in_specs=in_specs,
        out_specs=out_specs or ((VMEM,) * len(out_shape) if many else VMEM),
        scratch_shapes=list(scratch),
        compiler_params=pltpu.CompilerParams(vmem_limit_bytes=room << 20),
        cost_estimate=pl.CostEstimate(flops=1 << 20, transcendentals=0, bytes_accessed=1 << 18),
        name=name,
    )(*operands)


def split(value):
    high = value.astype(jnp.bfloat16)
    low = (value - high.astype(jnp.float32)).astype(jnp.bfloat16)
    return high, low


def dot3(a, b, dims):
    rows = a.shape[0]
    a_high, a_low = split(a)
    b_high, b_low = split(b)
    both = jnp.concatenate([a_high, a_low], axis=0)
    by_high = lax.dot_general(both, b_high, dims, preferred_element_type=jnp.float32)
    by_low = lax.dot_general(a_high, b_low, dims, preferred_element_type=jnp.float32)
    return by_high[:rows] + (by_high[rows:] + by_low)


def two_sum(a, b):
    total = a + b
    part = total - a
    return total, (a - (total - part)) + (b - part)


def two_product(a, b):
    def halves(x):
        big = x * 4097.0
        high = big - (big - x)
        return high, x - high

    product = a * b
    a_high, a_low = halves(a)
    b_high, b_low = halves(b)
    error = ((a_high * b_high - product) + a_high * b_low + a_low * b_high) + a_low * b_low
    return product, error


def pair_sum(a, b):
    total, error = two_sum(a[0], b[0])
    return two_sum(total, error + (a[1] + b[1]))


def pair_product(a, b):
    product, error = two_product(a[0], b[0])
    return two_sum(product, error + (a[0] * b[1] + a[1] * b[0]))


def scaled_pair(a, factor):
    return a[0] * factor, a[1] * factor


def lane_row(rows, lanes):
    return lax.broadcasted_iota(jnp.int32, (rows, lanes), 1)


def row_of(rows, lanes):
    return lax.broadcasted_iota(jnp.int32, (rows, lanes), 0)


def filled(pieces, rows):
    have = sum(piece.shape[1] for piece in pieces)
    return jnp.concatenate([*pieces, jnp.zeros((rows, LANES - have), jnp.float32)], axis=1)


def listed_row(corner_map):
    pieces = [corner_map[s : s + 1, :] for s in range(corner_map.shape[0])]
    have = sum(piece.shape[1] for piece in pieces)
    return jnp.concatenate([*pieces, jnp.full((1, LANES - have), -1, jnp.int32)], axis=1)


def start_kernel(
    loads_from, scaling_from, coupling_from, first, sent, stock, loads, scaling, coupling, arrived
):
    pairs = [(loads_from, loads), (scaling_from, scaling), (coupling_from, coupling)]
    copies = [pltpu.make_async_copy(*pair, arrived.at[i]) for i, pair in enumerate(pairs)]
    for copy in copies:
        copy.start()
    for copy in copies:
        copy.wait()
    subs, nrhs, _ = loads.shape
    corners = coupling.shape[1]
    parts = sent.shape[0]
    share = nrhs * CORES // parts
    norm = jnp.zeros((nrhs, 1), jnp.float32)
    sums, pairs = [], []
    for s in range(subs):
        scale = scaling[s : s + 1, :]
        scaled = scale * loads[s]
        first[s] = scaled
        stock[s, :nrhs, :] = loads[s]
        stock[s, nrhs : nrhs + corners, :] = coupling[s]
        stock[s, nrhs + corners :, :] = jnp.broadcast_to(scale, (SUBLANES, LANES))
        norm = norm + jnp.sum(loads[s] * scaled, axis=1, keepdims=True)
        sums.append(dot3(scaled, coupling[s], ROWS))
        pairs.append(dot3(coupling[s], scale * coupling[s], ROWS))
    wide = filled([*sums, norm], nrhs)
    pairs = filled(pairs, corners)
    for k in range(parts):
        y = k // CORES
        sent[k, :share, :] = wide[y * share : (y + 1) * share]
        sent[k, share:, :] = pairs


def choose_kernel(corner_map, inverse, out, pick):
    rows = inverse.shape[0]

    @pl.when(pl.program_id(0) == 0)
    def _():
        hit = row_of(*pick.shape) == listed_row(corner_map)
        pick[...] = jnp.where(hit, 1.0, 0.0).astype(jnp.bfloat16)

    both = jnp.concatenate(split(inverse[...]), axis=0)
    sums = lax.dot_general(both, pick[...], PLAIN, preferred_element_type=jnp.float32)
    out[...] = sums[:rows] + sums[rows:]


def choose(corner_map, inverse):
    rows, order = inverse.shape
    height = LANES
    return pl.pallas_call(
        choose_kernel,
        out_shape=f32(rows, LANES),
        grid=(rows // height,),
        in_specs=[
            pl.BlockSpec(corner_map.shape, lambda i: (0, 0)),
            pl.BlockSpec((height, order), lambda i: (i, 0)),
        ],
        out_specs=pl.BlockSpec((height, LANES), lambda i: (i, 0)),
        scratch_shapes=[pltpu.VMEM((order, LANES), jnp.bfloat16)],
        compiler_params=pltpu.CompilerParams(vmem_limit_bytes=12 << 20),
        name="choose",
    )(in_hbm(corner_map), in_hbm(inverse))


def first_message_kernel(place, stiffness, got, corner_map, out, kept):
    share = out.shape[1] - SUBLANES
    total = got[0]
    for k in range(1, got.shape[0]):
        total = total + got[k]
    kept[...] = total
    facts = [listed_row(corner_map).astype(jnp.float32)]
    for number in [place[i] for i in range(2)]:
        facts.append(jnp.full((1, LANES), number, jnp.int32).astype(jnp.float32))
    for s in range(stiffness.shape[0]):
        facts.append(jnp.full((1, LANES), stiffness[s], jnp.float32))
    facts.append(jnp.zeros((SUBLANES - len(facts), LANES), jnp.float32))
    facts = jnp.concatenate(facts, axis=0)
    for g in range(out.shape[0]):
        out[g, :share, :] = total[:share]
        out[g, share:, :] = facts


def coarse_kernel(listed, share, gathered, first_all, *refs):
    *refs, out, columns, arrived = refs
    ys = columns.shape[0]
    groups = gathered.shape[0]
    blocks = columns.shape[1] // LANES
    copies = [
        pltpu.make_async_copy(refs[d], columns.at[d], arrived.at[d]) for d in range(ys)
    ]
    for copy in copies:
        copy.start()
    half = ys * blocks * share
    y = first_all[0, share + 1 : share + 2, :].astype(jnp.int32)
    core = first_all[0, share + 2 : share + 3, :].astype(jnp.int32)
    sums = (jnp.zeros((share, LANES), jnp.float32),) * 2
    targets = [
        blocks * (CORES * lax.bitwise_and(y - d + ys, ys - 1) + core) + j
        for d in range(ys)
        for j in range(blocks)
    ]
    full = jnp.zeros((2 * half, LANES), jnp.float32)
    for pair in range(0, groups, 2):
        spread, pick = [], []
        for g in range(pair, pair + 2):
            corner = first_all[g, share : share + 1, :].astype(jnp.int32)
            high = lax.shift_right_arithmetic(corner, 7)
            low = lax.bitwise_and(corner, LANES - 1)
            mine = gathered[g, :share, :]
            most, rest = two_sum(sums[0], mine)
            sums = most, sums[1] + rest
            upper = mine.astype(jnp.bfloat16).astype(jnp.float32)
            lower = mine - upper
            rows = [jnp.where(high == target, x, 0.0) for x in (upper, lower) for target in targets]
            spread.append(jnp.concatenate(rows, axis=0).astype(jnp.bfloat16))
            at = row_of(LANES, LANES) == low
            pick.append(jnp.where(at, 1.0, 0.0).astype(jnp.bfloat16))
        full = full + lax.dot_general(
            jnp.concatenate(spread, axis=1),
            jnp.concatenate(pick, axis=1),
            ROWS,
            preferred_element_type=jnp.float32,
        )
    full = full[:half] + full[half:]
    total = jnp.zeros((share, LANES), jnp.float32)
    for copy in copies:
        copy.wait()
    for d in range(ys):
        row = d * blocks * share
        line = jnp.concatenate(
            [full[row + j * share : row + (j + 1) * share] for j in range(blocks)], axis=1
        )
        total = total + dot3(line, columns[d][...], PLAIN)
    lane = lane_row(share, LANES)
    most, rest = (jnp.sum(jnp.where(lane == listed, x, 0.0), axis=1, keepdims=True) for x in sums)
    answer = jnp.where(lane < listed, total, 0.0)
    total = answer + jnp.where(lane == listed, most / CORES, 0.0)
    total = total + jnp.where(lane == listed + 1, rest / CORES, 0.0)
    for k in range(out.shape[0]):
        out[k, :share, :] = total
    if len(refs) == ys:
        out[0, share:, :] = jnp.zeros((out.shape[1] - share, LANES), jnp.float32)
    else:
        near_part = refs[ys]
        for k in range(out.shape[0]):
            at = k // CORES * share
            out[k, share:, :] = near_part[near_part.shape[0] - 2, at : at + share, :]


def coarse_product(listed, share, gathered, first_all, columns, extra):
    operands = [gathered, first_all, *[in_hbm(part) for part in columns], *extra]
    return call(
        functools.partial(coarse_kernel, listed, share),
        "coarse_product",
        f32(CORES * len(columns) if extra else 1, 2 * share, LANES),
        [VMEM] * 2 + [ANY] * len(columns) + [VMEM] * len(extra),
        operands,
        [
            pltpu.VMEM((len(columns), *columns[0].shape), jnp.float32),
            pltpu.SemaphoreType.DMA((len(columns),)),
        ],
        room=10,
    )


def row_sums(products):
    nrhs, columns = products[0].shape
    width = len(products) * columns
    chosen = lax.div(lane_row(SUBLANES, width), columns) == row_of(SUBLANES, width)
    sums = lax.dot_general(
        jnp.where(chosen, 1.0, 0.0),
        jnp.concatenate(products, axis=1),
        ROWS,
        precision=HIGHEST,
        preferred_element_type=jnp.float32,
    )
    return jnp.concatenate([sums, jnp.zeros((SUBLANES, LANES - nrhs), jnp.float32)], axis=1)


def near_kernel(faces, share, with_sums, whole, schur, first_all, stock, *refs):
    if with_sums:
        *refs, out, line, after, before, contact, arrived = refs
    else:
        answer, rows, fields, *refs, out, sent, line, after, before, contact, arrived = refs
    *blocks, after_from, before_from, contact_from = refs
    subs, nrhs, columns = after.shape
    ys = len(blocks) // CORES
    corners = stock.shape[1] - nrhs - SUBLANES
    last = (2 * faces + 1) * subs
    y, core, group_after = whole[last], whole[last + 1], whole[last + 2]
    mine_at, partner_at = whole[last + 3], whole[last + 4]
    own = CORES * y + core
    pos = own * columns + lane_row(nrhs, columns)
    count = len(blocks)
    near_by = [(after_from, after), (before_from, before), (contact_from, contact)]
    near_by = [
        pltpu.make_async_copy(*pair, arrived.at[count + i]) for i, pair in enumerate(near_by)
    ]
    copies = []
    for i, block in enumerate(blocks):
        d, other = i % ys, i // ys
        chunk = CORES * lax.rem(y - d + ys, ys) + (1 - core if other else core)
        lanes = pl.ds(pl.multiple_of(chunk * columns, LANES), columns)
        copies.append(pltpu.make_async_copy(block, line.at[:, :, lanes], arrived.at[i]))
    for copy in [copies[0], *near_by, *copies[1:]]:
        copy.start()
    for copy in [copies[0], *near_by]:
        copy.wait()
    dots = jnp.zeros((nrhs, 1), jnp.float32)
    sums = []
    products = [jnp.zeros((nrhs, columns), jnp.float32)] * 2
    for s in range(subs):
        mine = line[s, :, pl.ds(pl.multiple_of(own * columns, LANES), columns)]
        at = lax.rem(whole[2 * faces * subs + s], subs)
        ours = first_all[mine_at, pl.ds(share + 3 + s, 1), :]
        theirs = first_all[partner_at, pl.ds(share + 3 + at, 1), :]
        total = (ours * theirs) * (mine - contact[at])
        for f in range(faces):
            target = whole[s * faces + f]
            at = lax.rem(target, subs)
            is_after = lax.div(target, subs) == group_after
            other = jnp.where(is_after, after[at], before[at])
            live = pos < whole[(subs + s) * faces + f]
            total = total + jnp.where(live, mine - other, 0.0)
        out[s] = total
    for copy in copies[1:]:
        copy.wait()
    for s in range(subs):
        mine = line[s, :, pl.ds(pl.multiple_of(own * columns, LANES), columns)]
        total = out[s] + dot3(line[s], schur[s], ROWS)
        out[s] = total
        if with_sums:
            dots = dots + jnp.sum(mine * total, axis=1, keepdims=True)
            scale = stock[s, nrhs + corners : nrhs + corners + 1, :]
            sums.append(dot3(scale * total, stock[s, nrhs : nrhs + corners, :], ROWS))
        else:
            products = [products[0] + mine * fields[subs + s], products[1] + mine * total]
    if with_sums:
        out[subs] = filled([*sums, dots], nrhs)
        out[subs + 1] = jnp.zeros((nrhs, LANES), jnp.float32)
    else:
        answer = answer[0, :share, :]
        ours = jnp.where(lane_row(share, LANES) < subs * corners, answer, 0.0)
        ones = jnp.ones((SUBLANES, LANES), jnp.float32)
        dots = lax.dot_general(
            ones,
            rows[nrhs:, :] * ours,
            ROWS,
            precision=HIGHEST,
            preferred_element_type=jnp.float32,
        )
        dots = jnp.concatenate([dots] * (LANES // share), axis=1)
        dots = jnp.where(lax.div(lane_row(SUBLANES, LANES), share) == y, dots, 0.0)
        dots = jnp.where(row_of(SUBLANES, LANES) == 1, dots, 0.0)
        dots = row_sums(products) + dots
        for k in range(sent.shape[0]):
            sent[k, :share, :] = answer
            sent[k, share:, :] = dots


def neighbourhood(field):
    ys = lax.axis_size("crs") // CORES
    same = [field] + [along_y(field, d) for d in range(1, ys)]
    cross = [other_core(part) for part in same]
    return (
        *same,
        *cross,
        along_sub(field, -1),
        along_sub(field, 1),
        along_sub(field, lax.axis_size("sub") // 2),
    )


def near_part(faces, share, whole, schur_blocks, first_all, stock, around, with_sums, *extra):
    subs, nrhs, columns = around[0].shape
    piece = pltpu.VMEM((subs, nrhs, columns), jnp.float32)
    return call(
        functools.partial(near_kernel, faces, share, with_sums),
        "near",
        f32(subs + 2, nrhs, columns)
        if with_sums
        else (
            f32(subs, nrhs, columns),
            f32(schur_blocks.shape[2] // columns, share + SUBLANES, LANES),
        ),
        [SMEM] + [VMEM] * (3 + len(extra)) + [ANY] * len(around),
        [whole, schur_blocks, first_all, stock, *extra, *[in_hbm(part) for part in around]],
        [
            pltpu.VMEM((subs, nrhs, schur_blocks.shape[2]), jnp.float32),
            piece,
            piece,
            piece,
            pltpu.SemaphoreType.DMA((len(around),)),
        ],
        room=8,
    )


def second_message_kernel(
    listed, got, kept, first_all, near_from, first_from, stock, out, second, fields, rows,
    near_first, first, message, arrived, left,
):
    subs = first.shape[0]
    pairs = [(near_from.at[pl.ds(0, subs)], near_first), (first_from, first)]
    fetches = [pltpu.make_async_copy(*pair, arrived.at[i]) for i, pair in enumerate(pairs)]
    for fetch in fetches:
        fetch.start()
    share = out.shape[1]
    parts = got.shape[0]
    subs, nrhs, _ = first.shape
    corners = kept.shape[0] - share
    y = first_all[0, share + 1 : share + 2, :].astype(jnp.int32)
    mine = jnp.zeros((share, LANES), jnp.float32)
    for k in range(parts // CORES):
        vals = got[CORES * k, :share, :] + got[CORES * k + 1, :share, :]
        rows[k * share : (k + 1) * share, :] = vals
        mine = jnp.where(y == k, vals, mine)
    total = got[0, share:, :]
    for k in range(1, parts):
        total = total + got[k, share:, :]
    pairs = kept[share:, :]
    copies = jnp.concatenate([pairs] * (listed // corners), axis=0)
    whose = lax.div(row_of(listed, LANES), corners) == lax.div(lane_row(listed, LANES), corners)
    copies = jnp.where(whose, copies, 0.0)
    total = total + dot3(mine[:, :listed], copies, PLAIN)
    lane = lane_row(share, LANES)
    curve = jnp.where(lane < listed, kept[:share, :] * mine, 0.0)
    curve = jnp.sum(curve, axis=1, keepdims=True)
    total = total + jnp.where(lane == listed, curve, 0.0)
    message[...] = total
    sends = [
        pltpu.make_async_copy(message, out.at[g], left.at[g]) for g in range(out.shape[0])
    ]
    for send in sends:
        send.start()
    rows[nrhs:, :] = total
    for fetch in fetches:
        fetch.wait()
    for s in range(subs):
        vals = rows[:nrhs, s * corners : (s + 1) * corners]
        image = near_first[s] + dot3(vals, stock[s, nrhs : nrhs + corners, :], PLAIN)
        scaled = stock[s, nrhs + corners : nrhs + corners + 1, :] * image
        second[s] = scaled
        fields[s] = first[s]
        fields[subs + s] = image
        fields[2 * subs + s] = scaled
    for send in sends:
        send.wait()


def last_message_kernel(got, out, vals):
    parts = got.shape[0]
    share = vals.shape[0] * CORES // parts
    total = got[0, share:, :]
    for k in range(1, parts):
        total = total + got[k, share:, :]
    for g in range(out.shape[0]):
        out[g] = total
    for k in range(parts // CORES):
        vals[k * share : (k + 1) * share, :] = (
            got[CORES * k, :share, :] + got[CORES * k + 1, :share, :]
        )


def last_field_kernel(vals, near_second, stock, out):
    nrhs = vals.shape[0]
    corners = stock.shape[1] - nrhs - SUBLANES
    for s in range(stock.shape[0]):
        out[s] = near_second[s] + dot3(
            vals[:, s * corners : (s + 1) * corners], stock[s, nrhs : nrhs + corners, :], PLAIN
        )


def last_kernel(listed, got, rows, vals, stock, fields, image_two, solution_out, residual_out):
    subs, nrhs, _ = image_two.shape
    total = got[0], jnp.zeros_like(got[0])
    for g in range(1, got.shape[0]):
        most, rest = two_sum(total[0], got[g])
        total = most, total[1] + rest
    same = jnp.where(row_of(nrhs, LANES) == lane_row(nrhs, LANES), 1.0, 0.0)
    columns = lax.dot_general(
        same,
        jnp.concatenate(total, axis=0),
        ROWS,
        precision=HIGHEST,
        preferred_element_type=jnp.float32,
    )
    at = listed
    norm = two_sum(rows[:nrhs, at : at + 1], rows[:nrhs, at + 1 : at + 2])
    curve = two_sum(vals[:, at : at + 1], vals[:, at + 1 : at + 2])
    cross = two_sum(columns[:, 0:1], columns[:, SUBLANES : SUBLANES + 1])
    last = two_sum(columns[:, 1:2], columns[:, SUBLANES + 1 : SUBLANES + 2])
    zero = jnp.zeros_like(norm[0])
    step = norm[0] / curve[0]
    wide = step, zero
    moved = pair_product(wide, cross)
    norm_next = pair_sum(
        norm, pair_product(wide, pair_sum(moved, scaled_pair(curve, -2.0)))
    )
    ratio = norm_next[0] / norm[0]
    more = two_sum(jnp.ones_like(ratio), ratio)
    curve_next = pair_product(more, pair_sum(pair_product(more, curve), scaled_pair(moved, -2.0)))
    curve_next = pair_sum(curve_next, pair_product(wide, pair_product(wide, last)))
    step_next = norm_next[0] / curve_next[0]
    for s in range(subs):
        first, image = fields[s], fields[subs + s]
        residual = stock[s, :nrhs, :] - step * image
        scaled = first - step * fields[2 * subs + s]
        scaled_image = image - step * image_two[s]
        solution_out[s] = step * first + step_next * (scaled + ratio * first)
        residual_out[s] = residual - step_next * (scaled_image + ratio * image)


def local(
    loads,
    schur_blocks,
    coupling,
    coarse_inverse,
    neighbours,
    face_len,
    contact_pair,
    stiffness,
    scaling,
    corner_map,
):
    sub_dev, nrhs, columns = loads.shape
    corners = coupling.shape[1]
    listed = sub_dev * corners
    groups = lax.axis_size("sub")
    parts = lax.axis_size("crs")
    ys = parts // CORES
    share = nrhs // ys
    field = f32(sub_dev, nrhs, columns)

    my_cols = lax.axis_index("crs")
    my_group = lax.axis_index("sub")
    place = jnp.stack(
        [
            my_cols // CORES,
            my_cols % CORES,
            (my_group + 1) % groups,
            my_group,
            (my_group + groups // 2) % groups,
        ]
    ).astype(jnp.int32)
    whole = jnp.concatenate([neighbours.reshape(-1), face_len.reshape(-1), contact_pair, place])

    first, sent, stock = call(
        start_kernel,
        "start",
        (
            field,
            f32(parts, share + corners, LANES),
            f32(sub_dev, nrhs + corners + SUBLANES, columns),
        ),
        [ANY] * 3,
        [in_hbm(loads), in_hbm(scaling), in_hbm(coupling)],
        [pltpu.VMEM(part.shape, jnp.float32) for part in (loads, scaling, coupling)]
        + [pltpu.SemaphoreType.DMA((3,))],
    )
    chosen = choose(after_all(corner_map, [sent]), coarse_inverse)
    got = after_all(exchange(sent, "crs"), [chosen])
    sent, kept = call(
        first_message_kernel,
        "first_message",
        (f32(groups, share + SUBLANES, LANES), f32(share + corners, LANES)),
        [SMEM] * 2 + [VMEM] * 2,
        [place, stiffness, got, corner_map],
    )
    chosen = after_all(chosen, [kept])
    inverse_cols = [chosen] + [along_y(chosen, d) for d in range(1, ys)]
    around = neighbourhood(after_all(first, [kept]))
    first_all = exchange(sent, "sub")
    near = functools.partial(
        near_part, neighbours.shape[1], share, whole, schur_blocks, first_all, stock
    )
    near_first = near(around, True)
    sent = coarse_product(listed, share, first_all, first_all, inverse_cols, (near_first,))
    got = exchange(sent, "crs")
    sent, second, fields, rows = call(
        functools.partial(second_message_kernel, listed),
        "second_message",
        (
            pltpu.HBM((groups, share, LANES), jnp.float32),
            field,
            f32(3 * sub_dev, nrhs, columns),
            f32(nrhs + share, LANES),
        ),
        [VMEM] * 3 + [ANY] * 2 + [VMEM],
        [got, kept, first_all, in_hbm(near_first), in_hbm(first), stock],
        [
            *[pltpu.VMEM((sub_dev, nrhs, columns), jnp.float32)] * 2,
            pltpu.VMEM((share, LANES), jnp.float32),
            pltpu.SemaphoreType.DMA((2,)),
            pltpu.SemaphoreType.DMA((groups,)),
        ],
        out_specs=(pl.BlockSpec(memory_space=pltpu.HBM), VMEM, VMEM, VMEM),
    )
    second_all = exchange(sent, "sub")
    around = neighbourhood(second)
    answer = coarse_product(listed, share, second_all, first_all, inverse_cols, ())
    near_second, sent = near(around, False, answer, rows, fields)
    got = exchange(sent, "crs")
    sent, vals = call(
        last_message_kernel,
        "last_message",
        (f32(groups, SUBLANES, LANES), f32(nrhs, LANES)),
        [VMEM],
        [got],
    )
    got = exchange(sent, "sub")
    image_two = call(last_field_kernel, "last_field", field, [VMEM] * 3, [vals, near_second, stock])
    return call(
        functools.partial(last_kernel, listed),
        "last",
        (field, field),
        [VMEM] * 6,
        [got, rows, vals, stock, fields, image_two],
    )


def solution(mesh):
    return jax.shard_map(
        local,
        mesh=mesh,
        in_specs=(
            P("sub", None, "crs"),
            P("sub", "crs", None),
            P("sub", None, "crs"),
            P("crs", None),
            P("sub", None),
            P("sub", None),
            P("sub"),
            P("sub"),
            P("sub", "crs"),
            P("sub", None),
        ),
        out_specs=(P("sub", None, "crs"), P("sub", None, "crs")),
        check_vma=False,
    )
```

```python
import functools

import jax
import jax.numpy as jnp
from jax import lax
from jax.experimental import pallas as pl
from jax.experimental.pallas import tpu as pltpu
from jax.sharding import PartitionSpec as P

HIGHEST = lax.Precision.HIGHEST
LANES = 128
SUBLANES = 8
CORES = 2
SMEM = pl.BlockSpec(memory_space=pltpu.SMEM)
VMEM = pl.BlockSpec(memory_space=pltpu.VMEM)
ANY = pl.BlockSpec(memory_space=pl.ANY)
ROWS = (((1,), (1,)), ((), ()))
PLAIN = (((1,), (0,)), ((), ()))


def along_sub(value, steps):
    count = lax.axis_size("sub")
    return lax.ppermute(value, "sub", [(s, (s + steps) % count) for s in range(count)])


def along_y(value, steps):
    count = lax.axis_size("crs")
    return lax.ppermute(value, "crs", [(s, (s + CORES * steps) % count) for s in range(count)])


def other_core(value):
    count = lax.axis_size("crs")
    return lax.ppermute(value, "crs", [(s, s ^ 1) for s in range(count)])


def exchange(value, axis):
    return lax.all_to_all(value, axis, 0, 0, tiled=True)


def after_all(value, others):
    return lax.optimization_barrier((value, *others))[0]


def in_hbm(value):
    return pltpu.with_memory_space_constraint(value, pltpu.HBM)


def after_all_of(values, others):
    return lax.optimization_barrier((tuple(values), *others))[0]


def f32(*shape):
    return jax.ShapeDtypeStruct(shape, jnp.float32)


def call(kernel, name, out_shape, in_specs, operands, scratch=(), room=4, out_specs=None):
    many = isinstance(out_shape, tuple)
    return pl.pallas_call(
        kernel,
        out_shape=out_shape,
        in_specs=in_specs,
        out_specs=out_specs or ((VMEM,) * len(out_shape) if many else VMEM),
        scratch_shapes=list(scratch),
        compiler_params=pltpu.CompilerParams(vmem_limit_bytes=room << 20),
        cost_estimate=pl.CostEstimate(flops=1 << 20, transcendentals=0, bytes_accessed=1 << 18),
        name=name,
    )(*operands)


def split(value):
    high = value.astype(jnp.bfloat16)
    low = (value - high.astype(jnp.float32)).astype(jnp.bfloat16)
    return high, low


def dot3(a, b, dims):
    return dot_split(a, *split(b), dims)


def dot_split(a, b_high, b_low, dims):
    rows = a.shape[0]
    a_high, a_low = split(a)
    both = jnp.concatenate([a_high, a_low], axis=0)
    by_high = lax.dot_general(both, b_high, dims, preferred_element_type=jnp.float32)
    by_low = lax.dot_general(a_high, b_low, dims, preferred_element_type=jnp.float32)
    return by_high[:rows] + (by_high[rows:] + by_low)


def two_sum(a, b):
    total = a + b
    part = total - a
    return total, (a - (total - part)) + (b - part)


def two_product(a, b):
    def halves(x):
        big = x * 4097.0
        high = big - (big - x)
        return high, x - high

    product = a * b
    a_high, a_low = halves(a)
    b_high, b_low = halves(b)
    error = ((a_high * b_high - product) + a_high * b_low + a_low * b_high) + a_low * b_low
    return product, error


def pair_sum(a, b):
    total, error = two_sum(a[0], b[0])
    return two_sum(total, error + (a[1] + b[1]))


def pair_product(a, b):
    product, error = two_product(a[0], b[0])
    return two_sum(product, error + (a[0] * b[1] + a[1] * b[0]))


def scaled_pair(a, factor):
    return a[0] * factor, a[1] * factor


def lane_row(rows, lanes):
    return lax.broadcasted_iota(jnp.int32, (rows, lanes), 1)


def row_of(rows, lanes):
    return lax.broadcasted_iota(jnp.int32, (rows, lanes), 0)


def filled(pieces, rows):
    have = sum(piece.shape[1] for piece in pieces)
    return jnp.concatenate([*pieces, jnp.zeros((rows, LANES - have), jnp.float32)], axis=1)


def listed_row(corner_map):
    pieces = [corner_map[s : s + 1, :] for s in range(corner_map.shape[0])]
    have = sum(piece.shape[1] for piece in pieces)
    return jnp.concatenate([*pieces, jnp.full((1, LANES - have), -1, jnp.int32)], axis=1)


def start_kernel(
    loads_from, scaling_from, coupling_from, first, sent, stock, loads, scaling, coupling, arrived
):
    pairs = [(loads_from, loads), (scaling_from, scaling), (coupling_from, coupling)]
    copies = [pltpu.make_async_copy(*pair, arrived.at[i]) for i, pair in enumerate(pairs)]
    for copy in copies:
        copy.start()
    for copy in copies:
        copy.wait()
    subs, nrhs, _ = loads.shape
    corners = coupling.shape[1]
    parts = sent.shape[0]
    share = nrhs * CORES // parts
    norm = jnp.zeros((nrhs, 1), jnp.float32)
    sums, pairs = [], []
    for s in range(subs):
        scale = scaling[s : s + 1, :]
        scaled = scale * loads[s]
        first[s] = scaled
        stock[s, :nrhs, :] = loads[s]
        stock[s, nrhs : nrhs + corners, :] = coupling[s]
        stock[s, nrhs + corners :, :] = jnp.broadcast_to(scale, (SUBLANES, LANES))
        norm = norm + jnp.sum(loads[s] * scaled, axis=1, keepdims=True)
        sums.append(dot3(scaled, coupling[s], ROWS))
        pairs.append(dot3(coupling[s], scale * coupling[s], ROWS))
    wide = filled([*sums, norm], nrhs)
    pairs = filled(pairs, corners)
    for k in range(parts):
        y = k // CORES
        sent[k, :share, :] = wide[y * share : (y + 1) * share]
        sent[k, share:, :] = pairs


def choose_kernel(corner_map, inverse, out, pick):
    rows = inverse.shape[0]

    @pl.when(pl.program_id(0) == 0)
    def _():
        hit = row_of(*pick.shape) == listed_row(corner_map)
        pick[...] = jnp.where(hit, 1.0, 0.0).astype(jnp.bfloat16)

    both = jnp.concatenate(split(inverse[...]), axis=0)
    sums = lax.dot_general(both, pick[...], PLAIN, preferred_element_type=jnp.float32)
    out[...] = sums[:rows] + sums[rows:]


def choose(corner_map, inverse):
    rows, order = inverse.shape
    height = rows // 2
    return pl.pallas_call(
        choose_kernel,
        out_shape=f32(rows, LANES),
        grid=(rows // height,),
        in_specs=[
            pl.BlockSpec(corner_map.shape, lambda i: (0, 0)),
            pl.BlockSpec((height, order), lambda i: (i, 0)),
        ],
        out_specs=pl.BlockSpec((height, LANES), lambda i: (i, 0)),
        scratch_shapes=[pltpu.VMEM((order, LANES), jnp.bfloat16)],
        compiler_params=pltpu.CompilerParams(vmem_limit_bytes=12 << 20),
        name="choose",
    )(in_hbm(corner_map), in_hbm(inverse))


def first_message_kernel(place, stiffness, got, corner_map, out, kept):
    share = out.shape[1] - SUBLANES
    total = got[0]
    for k in range(1, got.shape[0]):
        total = total + got[k]
    kept[...] = total
    facts = [listed_row(corner_map).astype(jnp.float32)]
    for number in [place[i] for i in range(2)]:
        facts.append(jnp.full((1, LANES), number, jnp.int32).astype(jnp.float32))
    for s in range(stiffness.shape[0]):
        facts.append(jnp.full((1, LANES), stiffness[s], jnp.float32))
    facts.append(jnp.zeros((SUBLANES - len(facts), LANES), jnp.float32))
    facts = jnp.concatenate(facts, axis=0)
    for g in range(out.shape[0]):
        out[g, :share, :] = total[:share]
        out[g, share:, :] = facts


def coarse_kernel(listed, share, gathered, first_all, *refs):
    *refs, out, columns, arrived = refs
    ys = columns.shape[0]
    groups = gathered.shape[0]
    blocks = columns.shape[1] // LANES
    copies = [
        pltpu.make_async_copy(refs[d], columns.at[d], arrived.at[d]) for d in range(ys)
    ]
    for copy in copies:
        copy.start()
    half = ys * blocks * share
    y = first_all[0, share + 1 : share + 2, :].astype(jnp.int32)
    core = first_all[0, share + 2 : share + 3, :].astype(jnp.int32)
    sums = (jnp.zeros((share, LANES), jnp.float32),) * 2
    targets = [
        blocks * (CORES * lax.bitwise_and(y - d + ys, ys - 1) + core) + j
        for d in range(ys)
        for j in range(blocks)
    ]
    full = jnp.zeros((2 * half, LANES), jnp.float32)
    for pair in range(0, groups, 2):
        spread, pick = [], []
        for g in range(pair, pair + 2):
            corner = first_all[g, share : share + 1, :].astype(jnp.int32)
            high = lax.shift_right_arithmetic(corner, 7)
            low = lax.bitwise_and(corner, LANES - 1)
            mine = gathered[g, :share, :]
            most, rest = two_sum(sums[0], mine)
            sums = most, sums[1] + rest
            upper = mine.astype(jnp.bfloat16).astype(jnp.float32)
            lower = mine - upper
            rows = [jnp.where(high == target, x, 0.0) for x in (upper, lower) for target in targets]
            spread.append(jnp.concatenate(rows, axis=0).astype(jnp.bfloat16))
            at = row_of(LANES, LANES) == low
            pick.append(jnp.where(at, 1.0, 0.0).astype(jnp.bfloat16))
        full = full + lax.dot_general(
            jnp.concatenate(spread, axis=1),
            jnp.concatenate(pick, axis=1),
            ROWS,
            preferred_element_type=jnp.float32,
        )
    full = full[:half] + full[half:]
    total = jnp.zeros((share, LANES), jnp.float32)
    for copy in copies:
        copy.wait()
    for d in range(ys):
        row = d * blocks * share
        line = jnp.concatenate(
            [full[row + j * share : row + (j + 1) * share] for j in range(blocks)], axis=1
        )
        total = total + dot3(line, columns[d][...], PLAIN)
    lane = lane_row(share, LANES)
    most, rest = (jnp.sum(jnp.where(lane == listed, x, 0.0), axis=1, keepdims=True) for x in sums)
    answer = jnp.where(lane < listed, total, 0.0)
    total = answer + jnp.where(lane == listed, most / CORES, 0.0)
    total = total + jnp.where(lane == listed + 1, rest / CORES, 0.0)
    for k in range(out.shape[0]):
        out[k, :share, :] = total
    if len(refs) == ys:
        out[0, share:, :] = jnp.zeros((out.shape[1] - share, LANES), jnp.float32)
    else:
        near_part = refs[ys]
        for k in range(out.shape[0]):
            at = k // CORES * share
            out[k, share:, :] = near_part[near_part.shape[0] - 2, at : at + share, :]


def coarse_product(listed, share, gathered, first_all, columns, extra):
    operands = [gathered, first_all, *[in_hbm(part) for part in columns], *extra]
    return call(
        functools.partial(coarse_kernel, listed, share),
        "coarse_product",
        f32(CORES * len(columns) if extra else 1, 2 * share, LANES),
        [VMEM] * 2 + [ANY] * len(columns) + [VMEM] * len(extra),
        operands,
        [
            pltpu.VMEM((len(columns), *columns[0].shape), jnp.float32),
            pltpu.SemaphoreType.DMA((len(columns),)),
        ],
        room=10,
    )


def row_sums(products):
    nrhs, columns = products[0].shape
    width = len(products) * columns
    chosen = lax.div(lane_row(SUBLANES, width), columns) == row_of(SUBLANES, width)
    sums = lax.dot_general(
        jnp.where(chosen, 1.0, 0.0),
        jnp.concatenate(products, axis=1),
        ROWS,
        precision=HIGHEST,
        preferred_element_type=jnp.float32,
    )
    return jnp.concatenate([sums, jnp.zeros((SUBLANES, LANES - nrhs), jnp.float32)], axis=1)


def near_kernel(faces, share, with_sums, whole, schur, first_all, stock, *refs):
    if with_sums:
        *refs, out, line, high, low, after, before, contact, arrived = refs
    else:
        answer, rows, fields, *refs, out, sent, line, high, low, after, before, contact, arrived = refs
    *blocks, after_from, before_from, contact_from = refs
    subs, nrhs, columns = after.shape
    ys = len(blocks) // CORES
    corners = stock.shape[1] - nrhs - SUBLANES
    last = 2 * faces + 1
    y, core, group_after, mine_at, partner_at = [whole[0, last + i] for i in range(5)]
    own = CORES * y + core
    pos = own * columns + lane_row(nrhs, columns)
    count = len(blocks)
    near_by = [(after_from, after), (before_from, before), (contact_from, contact)]
    near_by = [
        pltpu.make_async_copy(*pair, arrived.at[count + i]) for i, pair in enumerate(near_by)
    ]
    copies = []
    for i, block in enumerate(blocks):
        d, other = i % ys, i // ys
        chunk = CORES * lax.rem(y - d + ys, ys) + (1 - core if other else core)
        lanes = pl.ds(pl.multiple_of(chunk * columns, LANES), columns)
        copies.append(pltpu.make_async_copy(block, line.at[:, :, lanes], arrived.at[i]))
    for copy in [copies[0], *near_by, *copies[1:]]:
        copy.start()
    for s in range(subs):
        high[s], low[s] = split(schur[s])
    for copy in [copies[0], *near_by]:
        copy.wait()
    dots = jnp.zeros((nrhs, 1), jnp.float32)
    sums = []
    products = [jnp.zeros((nrhs, columns), jnp.float32)] * 2
    for s in range(subs):
        mine = line[s, :, pl.ds(pl.multiple_of(own * columns, LANES), columns)]
        at = lax.rem(whole[s, 2 * faces], subs)
        ours = first_all[mine_at, pl.ds(share + 3 + s, 1), :]
        theirs = first_all[partner_at, pl.ds(share + 3 + at, 1), :]
        total = (ours * theirs) * (mine - contact[at])
        for f in range(faces):
            target = whole[s, f]
            at = lax.rem(target, subs)
            is_after = lax.div(target, subs) == group_after
            other = jnp.where(is_after, after[at], before[at])
            live = pos < whole[s, faces + f]
            total = total + jnp.where(live, mine - other, 0.0)
        out[s] = total
    for copy in copies[1:]:
        copy.wait()
    for s in range(subs):
        mine = line[s, :, pl.ds(pl.multiple_of(own * columns, LANES), columns)]
        total = out[s] + dot_split(line[s], high[s], low[s], ROWS)
        out[s] = total
        if with_sums:
            dots = dots + jnp.sum(mine * total, axis=1, keepdims=True)
            scale = stock[s, nrhs + corners : nrhs + corners + 1, :]
            sums.append(dot3(scale * total, stock[s, nrhs : nrhs + corners, :], ROWS))
        else:
            products = [products[0] + mine * fields[subs + s], products[1] + mine * total]
    if with_sums:
        out[subs] = filled([*sums, dots], nrhs)
        out[subs + 1] = jnp.zeros((nrhs, LANES), jnp.float32)
    else:
        answer = answer[0, :share, :]
        ours = jnp.where(lane_row(share, LANES) < subs * corners, answer, 0.0)
        ones = jnp.ones((SUBLANES, LANES), jnp.float32)
        dots = lax.dot_general(
            ones,
            rows[nrhs:, :] * ours,
            ROWS,
            precision=HIGHEST,
            preferred_element_type=jnp.float32,
        )
        dots = jnp.concatenate([dots] * (LANES // share), axis=1)
        dots = jnp.where(lax.div(lane_row(SUBLANES, LANES), share) == y, dots, 0.0)
        dots = jnp.where(row_of(SUBLANES, LANES) == 1, dots, 0.0)
        dots = row_sums(products) + dots
        for k in range(sent.shape[0]):
            sent[k, :share, :] = answer
            sent[k, share:, :] = dots


def neighbourhood(field):
    ys = lax.axis_size("crs") // CORES
    same = [field] + [along_y(field, d) for d in range(1, ys)]
    cross = [other_core(part) for part in same]
    return (
        *same,
        *cross,
        along_sub(field, -1),
        along_sub(field, 1),
        along_sub(field, lax.axis_size("sub") // 2),
    )


def near_part(faces, share, whole, schur_blocks, first_all, stock, around, with_sums, *extra):
    subs, nrhs, columns = around[0].shape
    piece = pltpu.VMEM((subs, nrhs, columns), jnp.float32)
    return call(
        functools.partial(near_kernel, faces, share, with_sums),
        "near",
        f32(subs + 2, nrhs, columns)
        if with_sums
        else (
            f32(subs, nrhs, columns),
            f32(schur_blocks.shape[2] // columns, share + SUBLANES, LANES),
        ),
        [SMEM] + [VMEM] * (3 + len(extra)) + [ANY] * len(around),
        [whole, schur_blocks, first_all, stock, *extra, *[in_hbm(part) for part in around]],
        [
            pltpu.VMEM((subs, nrhs, schur_blocks.shape[2]), jnp.float32),
            pltpu.VMEM(schur_blocks.shape, jnp.bfloat16),
            pltpu.VMEM(schur_blocks.shape, jnp.bfloat16),
            piece,
            piece,
            piece,
            pltpu.SemaphoreType.DMA((len(around),)),
        ],
        room=8,
    )


def second_message_kernel(
    listed, got, kept, first_all, near_from, first_from, stock, out, second, fields, rows,
    near_first, first, message, arrived, left,
):
    subs = first.shape[0]
    pairs = [(near_from.at[pl.ds(0, subs)], near_first), (first_from, first)]
    fetches = [pltpu.make_async_copy(*pair, arrived.at[i]) for i, pair in enumerate(pairs)]
    for fetch in fetches:
        fetch.start()
    share = out.shape[1]
    parts = got.shape[0]
    subs, nrhs, _ = first.shape
    corners = kept.shape[0] - share
    y = first_all[0, share + 1 : share + 2, :].astype(jnp.int32)
    mine = jnp.zeros((share, LANES), jnp.float32)
    for k in range(parts // CORES):
        vals = got[CORES * k, :share, :] + got[CORES * k + 1, :share, :]
        rows[k * share : (k + 1) * share, :] = vals
        mine = jnp.where(y == k, vals, mine)
    total = got[0, share:, :]
    for k in range(1, parts):
        total = total + got[k, share:, :]
    pairs = kept[share:, :]
    copies = jnp.concatenate([pairs] * (listed // corners), axis=0)
    whose = lax.div(row_of(listed, LANES), corners) == lax.div(lane_row(listed, LANES), corners)
    copies = jnp.where(whose, copies, 0.0)
    total = total + dot3(mine[:, :listed], copies, PLAIN)
    lane = lane_row(share, LANES)
    curve = jnp.where(lane < listed, kept[:share, :] * mine, 0.0)
    curve = jnp.sum(curve, axis=1, keepdims=True)
    total = total + jnp.where(lane == listed, curve, 0.0)
    message[...] = total
    sends = [
        pltpu.make_async_copy(message, out.at[g], left.at[g]) for g in range(out.shape[0])
    ]
    for send in sends:
        send.start()
    rows[nrhs:, :] = total
    for fetch in fetches:
        fetch.wait()
    for s in range(subs):
        vals = rows[:nrhs, s * corners : (s + 1) * corners]
        image = near_first[s] + dot3(vals, stock[s, nrhs : nrhs + corners, :], PLAIN)
        scaled = stock[s, nrhs + corners : nrhs + corners + 1, :] * image
        second[s] = scaled
        fields[s] = first[s]
        fields[subs + s] = image
        fields[2 * subs + s] = scaled
    for send in sends:
        send.wait()


def last_message_kernel(got, out, vals):
    parts = got.shape[0]
    share = vals.shape[0] * CORES // parts
    total = got[0, share:, :]
    for k in range(1, parts):
        total = total + got[k, share:, :]
    for g in range(out.shape[0]):
        out[g] = total
    for k in range(parts // CORES):
        vals[k * share : (k + 1) * share, :] = (
            got[CORES * k, :share, :] + got[CORES * k + 1, :share, :]
        )


def last_field_kernel(vals, near_second, stock, out):
    nrhs = vals.shape[0]
    corners = stock.shape[1] - nrhs - SUBLANES
    for s in range(stock.shape[0]):
        out[s] = near_second[s] + dot3(
            vals[:, s * corners : (s + 1) * corners], stock[s, nrhs : nrhs + corners, :], PLAIN
        )


def last_kernel(listed, got, rows, vals, stock, fields, image_two, solution_out, residual_out):
    subs, nrhs, _ = image_two.shape
    total = got[0], jnp.zeros_like(got[0])
    for g in range(1, got.shape[0]):
        most, rest = two_sum(total[0], got[g])
        total = most, total[1] + rest
    same = jnp.where(row_of(nrhs, LANES) == lane_row(nrhs, LANES), 1.0, 0.0)
    columns = lax.dot_general(
        same,
        jnp.concatenate(total, axis=0),
        ROWS,
        precision=HIGHEST,
        preferred_element_type=jnp.float32,
    )
    at = listed
    norm = two_sum(rows[:nrhs, at : at + 1], rows[:nrhs, at + 1 : at + 2])
    curve = two_sum(vals[:, at : at + 1], vals[:, at + 1 : at + 2])
    cross = two_sum(columns[:, 0:1], columns[:, SUBLANES : SUBLANES + 1])
    last = two_sum(columns[:, 1:2], columns[:, SUBLANES + 1 : SUBLANES + 2])
    zero = jnp.zeros_like(norm[0])
    step = norm[0] / curve[0]
    wide = step, zero
    moved = pair_product(wide, cross)
    norm_next = pair_sum(
        norm, pair_product(wide, pair_sum(moved, scaled_pair(curve, -2.0)))
    )
    ratio = norm_next[0] / norm[0]
    more = two_sum(jnp.ones_like(ratio), ratio)
    curve_next = pair_product(more, pair_sum(pair_product(more, curve), scaled_pair(moved, -2.0)))
    curve_next = pair_sum(curve_next, pair_product(wide, pair_product(wide, last)))
    step_next = norm_next[0] / curve_next[0]
    for s in range(subs):
        first, image = fields[s], fields[subs + s]
        residual = stock[s, :nrhs, :] - step * image
        scaled = first - step * fields[2 * subs + s]
        scaled_image = image - step * image_two[s]
        solution_out[s] = step * first + step_next * (scaled + ratio * first)
        residual_out[s] = residual - step_next * (scaled_image + ratio * image)


def local(
    loads,
    schur_blocks,
    coupling,
    coarse_inverse,
    neighbours,
    face_len,
    contact_pair,
    stiffness,
    scaling,
    corner_map,
):
    sub_dev, nrhs, columns = loads.shape
    corners = coupling.shape[1]
    listed = sub_dev * corners
    groups = lax.axis_size("sub")
    parts = lax.axis_size("crs")
    ys = parts // CORES
    share = nrhs // ys
    field = f32(sub_dev, nrhs, columns)

    my_cols = lax.axis_index("crs")
    my_group = lax.axis_index("sub")
    place = jnp.stack(
        [
            my_cols // CORES,
            my_cols % CORES,
            (my_group + 1) % groups,
            my_group,
            (my_group + groups // 2) % groups,
        ]
    ).astype(jnp.int32)
    whole = jnp.concatenate(
        [
            neighbours,
            face_len,
            contact_pair[:, None],
            jnp.broadcast_to(place[None], (sub_dev, place.shape[0])),
        ],
        axis=1,
    )

    first, sent, stock = call(
        start_kernel,
        "start",
        (
            field,
            f32(parts, share + corners, LANES),
            f32(sub_dev, nrhs + corners + SUBLANES, columns),
        ),
        [ANY] * 3,
        [in_hbm(loads), in_hbm(scaling), in_hbm(coupling)],
        [pltpu.VMEM(part.shape, jnp.float32) for part in (loads, scaling, coupling)]
        + [pltpu.SemaphoreType.DMA((3,))],
    )
    chosen = choose(after_all(corner_map, [sent]), coarse_inverse)
    got = after_all(exchange(sent, "crs"), [chosen])
    sent, kept = call(
        first_message_kernel,
        "first_message",
        (f32(groups, share + SUBLANES, LANES), f32(share + corners, LANES)),
        [SMEM] * 2 + [VMEM] * 2,
        [place, stiffness, got, corner_map],
    )
    inverse_cols = [chosen] + [along_y(chosen, d) for d in range(1, ys)]
    around = neighbourhood(after_all(first, [kept]))
    first_all = exchange(sent, "sub")
    near = functools.partial(
        near_part, neighbours.shape[1], share, whole, schur_blocks, first_all, stock
    )
    around = (*around[:-3], *after_all_of(around[-3:], inverse_cols))
    near_first = near(around, True)
    sent = coarse_product(listed, share, first_all, first_all, inverse_cols, (near_first,))
    got = exchange(sent, "crs")
    sent, second, fields, rows = call(
        functools.partial(second_message_kernel, listed),
        "second_message",
        (
            pltpu.HBM((groups, share, LANES), jnp.float32),
            field,
            f32(3 * sub_dev, nrhs, columns),
            f32(nrhs + share, LANES),
        ),
        [VMEM] * 3 + [ANY] * 2 + [VMEM],
        [got, kept, first_all, in_hbm(near_first), in_hbm(first), stock],
        [
            *[pltpu.VMEM((sub_dev, nrhs, columns), jnp.float32)] * 2,
            pltpu.VMEM((share, LANES), jnp.float32),
            pltpu.SemaphoreType.DMA((2,)),
            pltpu.SemaphoreType.DMA((groups,)),
        ],
        out_specs=(pl.BlockSpec(memory_space=pltpu.HBM), VMEM, VMEM, VMEM),
    )
    second_all = exchange(sent, "sub")
    around = neighbourhood(second)
    answer = coarse_product(listed, share, second_all, first_all, inverse_cols, ())
    near_second, sent = near(around, False, answer, rows, fields)
    got = exchange(sent, "crs")
    sent, vals = call(
        last_message_kernel,
        "last_message",
        (f32(groups, SUBLANES, LANES), f32(nrhs, LANES)),
        [VMEM],
        [got],
    )
    got = exchange(sent, "sub")
    image_two = call(last_field_kernel, "last_field", field, [VMEM] * 3, [vals, near_second, stock])
    return call(
        functools.partial(last_kernel, listed),
        "last",
        (field, field),
        [VMEM] * 6,
        [got, rows, vals, stock, fields, image_two],
    )


def solution(mesh):
    return jax.shard_map(
        local,
        mesh=mesh,
        in_specs=(
            P("sub", None, "crs"),
            P("sub", "crs", None),
            P("sub", None, "crs"),
            P("crs", None),
            P("sub", None),
            P("sub", None),
            P("sub"),
            P("sub"),
            P("sub", "crs"),
            P("sub", None),
        ),
        out_specs=(P("sub", None, "crs"), P("sub", None, "crs")),
        check_vma=False,
    )
```

```python
import functools

import jax
import jax.numpy as jnp
from jax import lax
from jax.experimental import pallas as pl
from jax.experimental.pallas import tpu as pltpu
from jax.sharding import PartitionSpec as P

HIGHEST = lax.Precision.HIGHEST
LANES = 128
SUBLANES = 8
CORES = 2
SMEM = pl.BlockSpec(memory_space=pltpu.SMEM)
VMEM = pl.BlockSpec(memory_space=pltpu.VMEM)
ANY = pl.BlockSpec(memory_space=pl.ANY)
ROWS = (((1,), (1,)), ((), ()))
PLAIN = (((1,), (0,)), ((), ()))


def along_sub(value, steps):
    count = lax.axis_size("sub")
    return lax.ppermute(value, "sub", [(s, (s + steps) % count) for s in range(count)])


def along_y(value, steps):
    count = lax.axis_size("crs")
    return lax.ppermute(value, "crs", [(s, (s + CORES * steps) % count) for s in range(count)])


def other_core(value):
    count = lax.axis_size("crs")
    return lax.ppermute(value, "crs", [(s, s ^ 1) for s in range(count)])


def exchange(value, axis):
    return lax.all_to_all(value, axis, 0, 0, tiled=True)


def after_all(value, others):
    return lax.optimization_barrier((value, *others))[0]


def in_hbm(value):
    return pltpu.with_memory_space_constraint(value, pltpu.HBM)


def after_all_of(values, others):
    return lax.optimization_barrier((tuple(values), *others))[0]


def f32(*shape):
    return jax.ShapeDtypeStruct(shape, jnp.float32)


def call(kernel, name, out_shape, in_specs, operands, scratch=(), room=4, out_specs=None):
    many = isinstance(out_shape, tuple)
    return pl.pallas_call(
        kernel,
        out_shape=out_shape,
        in_specs=in_specs,
        out_specs=out_specs or ((VMEM,) * len(out_shape) if many else VMEM),
        scratch_shapes=list(scratch),
        compiler_params=pltpu.CompilerParams(vmem_limit_bytes=room << 20),
        cost_estimate=pl.CostEstimate(flops=1 << 20, transcendentals=0, bytes_accessed=1 << 18),
        name=name,
    )(*operands)


def split(value):
    high = value.astype(jnp.bfloat16)
    low = (value - high.astype(jnp.float32)).astype(jnp.bfloat16)
    return high, low


def dot3(a, b, dims):
    return dot_split(a, *split(b), dims)


def dot_split(a, b_high, b_low, dims):
    rows = a.shape[0]
    a_high, a_low = split(a)
    both = jnp.concatenate([a_high, a_low], axis=0)
    by_high = lax.dot_general(both, b_high, dims, preferred_element_type=jnp.float32)
    by_low = lax.dot_general(a_high, b_low, dims, preferred_element_type=jnp.float32)
    return by_high[:rows] + (by_high[rows:] + by_low)


def two_sum(a, b):
    total = a + b
    part = total - a
    return total, (a - (total - part)) + (b - part)


def two_product(a, b):
    def halves(x):
        big = x * 4097.0
        high = big - (big - x)
        return high, x - high

    product = a * b
    a_high, a_low = halves(a)
    b_high, b_low = halves(b)
    error = ((a_high * b_high - product) + a_high * b_low + a_low * b_high) + a_low * b_low
    return product, error


def pair_sum(a, b):
    total, error = two_sum(a[0], b[0])
    return two_sum(total, error + (a[1] + b[1]))


def pair_product(a, b):
    product, error = two_product(a[0], b[0])
    return two_sum(product, error + (a[0] * b[1] + a[1] * b[0]))


def scaled_pair(a, factor):
    return a[0] * factor, a[1] * factor


def lane_row(rows, lanes):
    return lax.broadcasted_iota(jnp.int32, (rows, lanes), 1)


def row_of(rows, lanes):
    return lax.broadcasted_iota(jnp.int32, (rows, lanes), 0)


def filled(pieces, rows):
    have = sum(piece.shape[1] for piece in pieces)
    return jnp.concatenate([*pieces, jnp.zeros((rows, LANES - have), jnp.float32)], axis=1)


def listed_row(corner_map):
    pieces = [corner_map[s : s + 1, :] for s in range(corner_map.shape[0])]
    have = sum(piece.shape[1] for piece in pieces)
    return jnp.concatenate([*pieces, jnp.full((1, LANES - have), -1, jnp.int32)], axis=1)


def start_kernel(
    loads_from, scaling_from, coupling_from, first, sent, stock, loads, scaling, coupling, arrived
):
    pairs = [(loads_from, loads), (scaling_from, scaling), (coupling_from, coupling)]
    copies = [pltpu.make_async_copy(*pair, arrived.at[i]) for i, pair in enumerate(pairs)]
    for copy in copies:
        copy.start()
    for copy in copies:
        copy.wait()
    subs, nrhs, _ = loads.shape
    corners = coupling.shape[1]
    parts = sent.shape[0]
    share = nrhs * CORES // parts
    norm = jnp.zeros((nrhs, 1), jnp.float32)
    sums, pairs = [], []
    for s in range(subs):
        scale = scaling[s : s + 1, :]
        scaled = scale * loads[s]
        first[s] = scaled
        stock[s, :nrhs, :] = loads[s]
        stock[s, nrhs : nrhs + corners, :] = coupling[s]
        stock[s, nrhs + corners :, :] = jnp.broadcast_to(scale, (SUBLANES, LANES))
        norm = norm + jnp.sum(loads[s] * scaled, axis=1, keepdims=True)
        sums.append(dot3(scaled, coupling[s], ROWS))
        pairs.append(dot3(coupling[s], scale * coupling[s], ROWS))
    wide = filled([*sums, norm], nrhs)
    pairs = filled(pairs, corners)
    for k in range(parts):
        y = k // CORES
        sent[k, :share, :] = wide[y * share : (y + 1) * share]
        sent[k, share:, :] = pairs


def choose_kernel(corner_map, inverse, out, pick):
    rows = inverse.shape[0]

    @pl.when(pl.program_id(0) == 0)
    def _():
        hit = row_of(*pick.shape) == listed_row(corner_map)
        pick[...] = jnp.where(hit, 1.0, 0.0).astype(jnp.bfloat16)

    both = jnp.concatenate(split(inverse[...]), axis=0)
    sums = lax.dot_general(both, pick[...], PLAIN, preferred_element_type=jnp.float32)
    out[...] = sums[:rows] + sums[rows:]


def choose(corner_map, inverse):
    rows, order = inverse.shape
    height = rows // 2
    return pl.pallas_call(
        choose_kernel,
        out_shape=f32(rows, LANES),
        grid=(rows // height,),
        in_specs=[
            pl.BlockSpec(corner_map.shape, lambda i: (0, 0)),
            pl.BlockSpec((height, order), lambda i: (i, 0)),
        ],
        out_specs=pl.BlockSpec((height, LANES), lambda i: (i, 0)),
        scratch_shapes=[pltpu.VMEM((order, LANES), jnp.bfloat16)],
        compiler_params=pltpu.CompilerParams(vmem_limit_bytes=12 << 20),
        name="choose",
    )(in_hbm(corner_map), in_hbm(inverse))


def first_message_kernel(place, stiffness, got, corner_map, out, kept):
    share = out.shape[1] - SUBLANES
    total = got[0]
    for k in range(1, got.shape[0]):
        total = total + got[k]
    kept[...] = total
    facts = [listed_row(corner_map).astype(jnp.float32)]
    for number in [place[i] for i in range(2)]:
        facts.append(jnp.full((1, LANES), number, jnp.int32).astype(jnp.float32))
    for s in range(stiffness.shape[0]):
        facts.append(jnp.full((1, LANES), stiffness[s], jnp.float32))
    facts.append(jnp.zeros((SUBLANES - len(facts), LANES), jnp.float32))
    facts = jnp.concatenate(facts, axis=0)
    for g in range(out.shape[0]):
        out[g, :share, :] = total[:share]
        out[g, share:, :] = facts


def coarse_kernel(listed, share, gathered, first_all, *refs):
    *refs, out, columns, arrived = refs
    ys = columns.shape[0]
    groups = gathered.shape[0]
    blocks = columns.shape[1] // LANES
    copies = [
        pltpu.make_async_copy(refs[d], columns.at[d], arrived.at[d]) for d in range(ys)
    ]
    for copy in copies:
        copy.start()
    half = ys * blocks * share
    y = first_all[0, share + 1 : share + 2, :].astype(jnp.int32)
    core = first_all[0, share + 2 : share + 3, :].astype(jnp.int32)
    sums = (jnp.zeros((share, LANES), jnp.float32),) * 2
    targets = [
        blocks * (CORES * lax.bitwise_and(y - d + ys, ys - 1) + core) + j
        for d in range(ys)
        for j in range(blocks)
    ]
    full = jnp.zeros((2 * half, LANES), jnp.float32)
    for pair in range(0, groups, 4):
        spread, pick = [], []
        for g in range(pair, pair + 4):
            corner = first_all[g, share : share + 1, :].astype(jnp.int32)
            high = lax.shift_right_arithmetic(corner, 7)
            low = lax.bitwise_and(corner, LANES - 1)
            mine = gathered[g, :share, :]
            most, rest = two_sum(sums[0], mine)
            sums = most, sums[1] + rest
            upper = mine.astype(jnp.bfloat16).astype(jnp.float32)
            lower = mine - upper
            rows = [jnp.where(high == target, x, 0.0) for x in (upper, lower) for target in targets]
            spread.append(jnp.concatenate(rows, axis=0).astype(jnp.bfloat16))
            at = row_of(LANES, LANES) == low
            pick.append(jnp.where(at, 1.0, 0.0).astype(jnp.bfloat16))
        full = full + lax.dot_general(
            jnp.concatenate(spread, axis=1),
            jnp.concatenate(pick, axis=1),
            ROWS,
            preferred_element_type=jnp.float32,
        )
    full = full[:half] + full[half:]
    total = jnp.zeros((share, LANES), jnp.float32)
    for copy in copies:
        copy.wait()
    for d in range(ys):
        row = d * blocks * share
        line = jnp.concatenate(
            [full[row + j * share : row + (j + 1) * share] for j in range(blocks)], axis=1
        )
        total = total + dot3(line, columns[d][...], PLAIN)
    lane = lane_row(share, LANES)
    most, rest = (jnp.sum(jnp.where(lane == listed, x, 0.0), axis=1, keepdims=True) for x in sums)
    answer = jnp.where(lane < listed, total, 0.0)
    total = answer + jnp.where(lane == listed, most / CORES, 0.0)
    total = total + jnp.where(lane == listed + 1, rest / CORES, 0.0)
    for k in range(out.shape[0]):
        out[k, :share, :] = total
    if len(refs) == ys:
        out[0, share:, :] = jnp.zeros((out.shape[1] - share, LANES), jnp.float32)
    else:
        near_part = refs[ys]
        for k in range(out.shape[0]):
            at = k // CORES * share
            out[k, share:, :] = near_part[near_part.shape[0] - 2, at : at + share, :]


def coarse_product(listed, share, gathered, first_all, columns, extra):
    operands = [gathered, first_all, *[in_hbm(part) for part in columns], *extra]
    return call(
        functools.partial(coarse_kernel, listed, share),
        "coarse_product",
        f32(CORES * len(columns) if extra else 1, 2 * share, LANES),
        [VMEM] * 2 + [ANY] * len(columns) + [VMEM] * len(extra),
        operands,
        [
            pltpu.VMEM((len(columns), *columns[0].shape), jnp.float32),
            pltpu.SemaphoreType.DMA((len(columns),)),
        ],
        room=10,
    )


def row_sums(products):
    nrhs, columns = products[0].shape
    width = len(products) * columns
    chosen = lax.div(lane_row(SUBLANES, width), columns) == row_of(SUBLANES, width)
    sums = lax.dot_general(
        jnp.where(chosen, 1.0, 0.0),
        jnp.concatenate(products, axis=1),
        ROWS,
        precision=HIGHEST,
        preferred_element_type=jnp.float32,
    )
    return jnp.concatenate([sums, jnp.zeros((SUBLANES, LANES - nrhs), jnp.float32)], axis=1)


def near_kernel(faces, share, with_sums, whole, schur, first_all, stock, *refs):
    if with_sums:
        *refs, out, line, high, low, after, before, contact, arrived = refs
    else:
        answer, rows, fields, *refs, out, sent, line, high, low, after, before, contact, arrived = refs
    *blocks, after_from, before_from, contact_from = refs
    subs, nrhs, columns = after.shape
    ys = len(blocks) // CORES
    corners = stock.shape[1] - nrhs - SUBLANES
    last = 2 * faces + 1
    y, core, group_after, mine_at, partner_at = [whole[0, last + i] for i in range(5)]
    own = CORES * y + core
    pos = own * columns + lane_row(nrhs, columns)
    count = len(blocks)
    near_by = [(after_from, after), (before_from, before), (contact_from, contact)]
    near_by = [
        pltpu.make_async_copy(*pair, arrived.at[count + i]) for i, pair in enumerate(near_by)
    ]
    copies = []
    for i, block in enumerate(blocks):
        d, other = i % ys, i // ys
        chunk = CORES * lax.rem(y - d + ys, ys) + (1 - core if other else core)
        lanes = pl.ds(pl.multiple_of(chunk * columns, LANES), columns)
        copies.append(pltpu.make_async_copy(block, line.at[:, :, lanes], arrived.at[i]))
    for copy in [copies[0], *near_by, *copies[1:]]:
        copy.start()
    for s in range(subs):
        high[s], low[s] = split(schur[s])
    for copy in [copies[0], *near_by]:
        copy.wait()
    dots = jnp.zeros((nrhs, 1), jnp.float32)
    sums = []
    products = [jnp.zeros((nrhs, columns), jnp.float32)] * 2
    for s in range(subs):
        mine = line[s, :, pl.ds(pl.multiple_of(own * columns, LANES), columns)]
        at = lax.rem(whole[s, 2 * faces], subs)
        ours = first_all[mine_at, pl.ds(share + 3 + s, 1), :]
        theirs = first_all[partner_at, pl.ds(share + 3 + at, 1), :]
        total = (ours * theirs) * (mine - contact[at])
        for f in range(faces):
            target = whole[s, f]
            at = lax.rem(target, subs)
            is_after = lax.div(target, subs) == group_after
            other = jnp.where(is_after, after[at], before[at])
            live = pos < whole[s, faces + f]
            total = total + jnp.where(live, mine - other, 0.0)
        out[s] = total
    for copy in copies[1:]:
        copy.wait()
    for s in range(subs):
        mine = line[s, :, pl.ds(pl.multiple_of(own * columns, LANES), columns)]
        total = out[s] + dot_split(line[s], high[s], low[s], ROWS)
        out[s] = total
        if with_sums:
            dots = dots + jnp.sum(mine * total, axis=1, keepdims=True)
            scale = stock[s, nrhs + corners : nrhs + corners + 1, :]
            sums.append(dot3(scale * total, stock[s, nrhs : nrhs + corners, :], ROWS))
        else:
            products = [products[0] + mine * fields[subs + s], products[1] + mine * total]
    if with_sums:
        out[subs] = filled([*sums, dots], nrhs)
        out[subs + 1] = jnp.zeros((nrhs, LANES), jnp.float32)
    else:
        answer = answer[0, :share, :]
        ours = jnp.where(lane_row(share, LANES) < subs * corners, answer, 0.0)
        ones = jnp.ones((SUBLANES, LANES), jnp.float32)
        dots = lax.dot_general(
            ones,
            rows[nrhs:, :] * ours,
            ROWS,
            precision=HIGHEST,
            preferred_element_type=jnp.float32,
        )
        dots = jnp.concatenate([dots] * (LANES // share), axis=1)
        dots = jnp.where(lax.div(lane_row(SUBLANES, LANES), share) == y, dots, 0.0)
        dots = jnp.where(row_of(SUBLANES, LANES) == 1, dots, 0.0)
        dots = row_sums(products) + dots
        for k in range(sent.shape[0]):
            sent[k, :share, :] = answer
            sent[k, share:, :] = dots


def neighbourhood(field):
    ys = lax.axis_size("crs") // CORES
    same = [field] + [along_y(field, d) for d in range(1, ys)]
    cross = [other_core(part) for part in same]
    return (
        *same,
        *cross,
        along_sub(field, -1),
        along_sub(field, 1),
        along_sub(field, lax.axis_size("sub") // 2),
    )


def near_part(faces, share, whole, schur_blocks, first_all, stock, around, with_sums, *extra):
    subs, nrhs, columns = around[0].shape
    piece = pltpu.VMEM((subs, nrhs, columns), jnp.float32)
    return call(
        functools.partial(near_kernel, faces, share, with_sums),
        "near",
        f32(subs + 2, nrhs, columns)
        if with_sums
        else (
            f32(subs, nrhs, columns),
            f32(schur_blocks.shape[2] // columns, share + SUBLANES, LANES),
        ),
        [SMEM] + [VMEM] * (3 + len(extra)) + [ANY] * len(around),
        [whole, schur_blocks, first_all, stock, *extra, *[in_hbm(part) for part in around]],
        [
            pltpu.VMEM((subs, nrhs, schur_blocks.shape[2]), jnp.float32),
            pltpu.VMEM(schur_blocks.shape, jnp.bfloat16),
            pltpu.VMEM(schur_blocks.shape, jnp.bfloat16),
            piece,
            piece,
            piece,
            pltpu.SemaphoreType.DMA((len(around),)),
        ],
        room=8,
    )


def second_message_kernel(
    listed, got, kept, first_all, near_from, first_from, stock, out, second, fields, rows,
    near_first, first, message, arrived, left,
):
    subs = first.shape[0]
    pairs = [(near_from.at[pl.ds(0, subs)], near_first), (first_from, first)]
    fetches = [pltpu.make_async_copy(*pair, arrived.at[i]) for i, pair in enumerate(pairs)]
    for fetch in fetches:
        fetch.start()
    share = out.shape[1]
    parts = got.shape[0]
    subs, nrhs, _ = first.shape
    corners = kept.shape[0] - share
    y = first_all[0, share + 1 : share + 2, :].astype(jnp.int32)
    mine = jnp.zeros((share, LANES), jnp.float32)
    for k in range(parts // CORES):
        vals = got[CORES * k, :share, :] + got[CORES * k + 1, :share, :]
        rows[k * share : (k + 1) * share, :] = vals
        mine = jnp.where(y == k, vals, mine)
    total = got[0, share:, :]
    for k in range(1, parts):
        total = total + got[k, share:, :]
    pairs = kept[share:, :]
    copies = jnp.concatenate([pairs] * (listed // corners), axis=0)
    whose = lax.div(row_of(listed, LANES), corners) == lax.div(lane_row(listed, LANES), corners)
    copies = jnp.where(whose, copies, 0.0)
    total = total + dot3(mine[:, :listed], copies, PLAIN)
    lane = lane_row(share, LANES)
    curve = jnp.where(lane < listed, kept[:share, :] * mine, 0.0)
    curve = jnp.sum(curve, axis=1, keepdims=True)
    total = total + jnp.where(lane == listed, curve, 0.0)
    message[...] = total
    sends = [
        pltpu.make_async_copy(message, out.at[g], left.at[g]) for g in range(out.shape[0])
    ]
    for send in sends:
        send.start()
    rows[nrhs:, :] = total
    for fetch in fetches:
        fetch.wait()
    for s in range(subs):
        vals = rows[:nrhs, s * corners : (s + 1) * corners]
        image = near_first[s] + dot3(vals, stock[s, nrhs : nrhs + corners, :], PLAIN)
        scaled = stock[s, nrhs + corners : nrhs + corners + 1, :] * image
        second[s] = scaled
        fields[s] = first[s]
        fields[subs + s] = image
        fields[2 * subs + s] = scaled
    for send in sends:
        send.wait()


def last_message_kernel(got, out, vals):
    parts = got.shape[0]
    share = vals.shape[0] * CORES // parts
    total = got[0, share:, :]
    for k in range(1, parts):
        total = total + got[k, share:, :]
    for g in range(out.shape[0]):
        out[g] = total
    for k in range(parts // CORES):
        vals[k * share : (k + 1) * share, :] = (
            got[CORES * k, :share, :] + got[CORES * k + 1, :share, :]
        )


def last_field_kernel(vals, near_second, stock, out):
    nrhs = vals.shape[0]
    corners = stock.shape[1] - nrhs - SUBLANES
    for s in range(stock.shape[0]):
        out[s] = near_second[s] + dot3(
            vals[:, s * corners : (s + 1) * corners], stock[s, nrhs : nrhs + corners, :], PLAIN
        )


def last_kernel(listed, got, rows, vals, stock, fields, image_two, solution_out, residual_out):
    subs, nrhs, _ = image_two.shape
    total = got[0], jnp.zeros_like(got[0])
    for g in range(1, got.shape[0]):
        most, rest = two_sum(total[0], got[g])
        total = most, total[1] + rest
    same = jnp.where(row_of(nrhs, LANES) == lane_row(nrhs, LANES), 1.0, 0.0)
    columns = lax.dot_general(
        same,
        jnp.concatenate(total, axis=0),
        ROWS,
        precision=HIGHEST,
        preferred_element_type=jnp.float32,
    )
    at = listed
    norm = two_sum(rows[:nrhs, at : at + 1], rows[:nrhs, at + 1 : at + 2])
    curve = two_sum(vals[:, at : at + 1], vals[:, at + 1 : at + 2])
    cross = two_sum(columns[:, 0:1], columns[:, SUBLANES : SUBLANES + 1])
    last = two_sum(columns[:, 1:2], columns[:, SUBLANES + 1 : SUBLANES + 2])
    zero = jnp.zeros_like(norm[0])
    step = norm[0] / curve[0]
    wide = step, zero
    moved = pair_product(wide, cross)
    norm_next = pair_sum(
        norm, pair_product(wide, pair_sum(moved, scaled_pair(curve, -2.0)))
    )
    ratio = norm_next[0] / norm[0]
    more = two_sum(jnp.ones_like(ratio), ratio)
    curve_next = pair_product(more, pair_sum(pair_product(more, curve), scaled_pair(moved, -2.0)))
    curve_next = pair_sum(curve_next, pair_product(wide, pair_product(wide, last)))
    step_next = norm_next[0] / curve_next[0]
    for s in range(subs):
        first, image = fields[s], fields[subs + s]
        residual = stock[s, :nrhs, :] - step * image
        scaled = first - step * fields[2 * subs + s]
        scaled_image = image - step * image_two[s]
        solution_out[s] = step * first + step_next * (scaled + ratio * first)
        residual_out[s] = residual - step_next * (scaled_image + ratio * image)


def local(
    loads,
    schur_blocks,
    coupling,
    coarse_inverse,
    neighbours,
    face_len,
    contact_pair,
    stiffness,
    scaling,
    corner_map,
):
    sub_dev, nrhs, columns = loads.shape
    corners = coupling.shape[1]
    listed = sub_dev * corners
    groups = lax.axis_size("sub")
    parts = lax.axis_size("crs")
    ys = parts // CORES
    share = nrhs // ys
    field = f32(sub_dev, nrhs, columns)

    my_cols = lax.axis_index("crs")
    my_group = lax.axis_index("sub")
    place = jnp.stack(
        [
            my_cols // CORES,
            my_cols % CORES,
            (my_group + 1) % groups,
            my_group,
            (my_group + groups // 2) % groups,
        ]
    ).astype(jnp.int32)
    whole = jnp.concatenate(
        [
            neighbours,
            face_len,
            contact_pair[:, None],
            jnp.broadcast_to(place[None], (sub_dev, place.shape[0])),
        ],
        axis=1,
    )

    first, sent, stock = call(
        start_kernel,
        "start",
        (
            field,
            f32(parts, share + corners, LANES),
            f32(sub_dev, nrhs + corners + SUBLANES, columns),
        ),
        [ANY] * 3,
        [in_hbm(loads), in_hbm(scaling), in_hbm(coupling)],
        [pltpu.VMEM(part.shape, jnp.float32) for part in (loads, scaling, coupling)]
        + [pltpu.SemaphoreType.DMA((3,))],
    )
    chosen = choose(after_all(corner_map, [sent]), coarse_inverse)
    got = after_all(exchange(sent, "crs"), [chosen])
    sent, kept = call(
        first_message_kernel,
        "first_message",
        (f32(groups, share + SUBLANES, LANES), f32(share + corners, LANES)),
        [SMEM] * 2 + [VMEM] * 2,
        [place, stiffness, got, corner_map],
    )
    inverse_cols = [chosen] + [along_y(chosen, d) for d in range(1, ys)]
    around = neighbourhood(after_all(first, [kept]))
    first_all = exchange(sent, "sub")
    near = functools.partial(
        near_part, neighbours.shape[1], share, whole, schur_blocks, first_all, stock
    )
    around = (*around[:-3], *after_all_of(around[-3:], inverse_cols))
    near_first = near(around, True)
    sent = coarse_product(listed, share, first_all, first_all, inverse_cols, (near_first,))
    got = exchange(sent, "crs")
    sent, second, fields, rows = call(
        functools.partial(second_message_kernel, listed),
        "second_message",
        (
            pltpu.HBM((groups, share, LANES), jnp.float32),
            field,
            f32(3 * sub_dev, nrhs, columns),
            f32(nrhs + share, LANES),
        ),
        [VMEM] * 3 + [ANY] * 2 + [VMEM],
        [got, kept, first_all, in_hbm(near_first), in_hbm(first), stock],
        [
            *[pltpu.VMEM((sub_dev, nrhs, columns), jnp.float32)] * 2,
            pltpu.VMEM((share, LANES), jnp.float32),
            pltpu.SemaphoreType.DMA((2,)),
            pltpu.SemaphoreType.DMA((groups,)),
        ],
        out_specs=(pl.BlockSpec(memory_space=pltpu.HBM), VMEM, VMEM, VMEM),
    )
    second_all = exchange(sent, "sub")
    around = neighbourhood(second)
    answer = coarse_product(listed, share, second_all, first_all, inverse_cols, ())
    near_second, sent = near(around, False, answer, rows, fields)
    got = exchange(sent, "crs")
    sent, vals = call(
        last_message_kernel,
        "last_message",
        (f32(groups, SUBLANES, LANES), f32(nrhs, LANES)),
        [VMEM],
        [got],
    )
    got = exchange(sent, "sub")
    image_two = call(last_field_kernel, "last_field", field, [VMEM] * 3, [vals, near_second, stock])
    return call(
        functools.partial(last_kernel, listed),
        "last",
        (field, field),
        [VMEM] * 6,
        [got, rows, vals, stock, fields, image_two],
    )


def solution(mesh):
    return jax.shard_map(
        local,
        mesh=mesh,
        in_specs=(
            P("sub", None, "crs"),
            P("sub", "crs", None),
            P("sub", None, "crs"),
            P("crs", None),
            P("sub", None),
            P("sub", None),
            P("sub"),
            P("sub"),
            P("sub", "crs"),
            P("sub", None),
        ),
        out_specs=(P("sub", None, "crs"), P("sub", None, "crs")),
        check_vma=False,
    )
```
